128 devices in a mesh: node: 32 (over z, y_lo, x), rep: 4 (over y_hi, core).
Axes of the slice: x: 4, y: 4 (y_hi: 2, y_lo: 2; y = y_hi * 2 + y_lo), z: 4, core: 2. Of those that a mesh axis runs over, the one named last changes fastest.
Arguments:
- node_feats: bfloat16 [65536, 256], P('node'), may hold values from -6 to 6
- weight: bfloat16 [256, 256], replicated, may hold values from -0.375 to 0.375
- cotangent: bfloat16 [65536, 256], P(('node', 'rep')), may hold values from -6 to 6
- tiles: bfloat16 [32, 4, 160, 256, 256], P('node', 'rep'), may hold values from -0.049804688 to 0.049804688
- tile_rows: int32 [32, 4, 160], P('node', 'rep'), may hold values from 0 to 7
- tile_cols: int32 [32, 4, 160], P('node', 'rep'), may hold values from 0 to 63
- tile_count: int32 [32, 4], P('node', 'rep'), may hold values from 80 to 160, as said below
Outputs:
- activated: bfloat16 [65536, 256], P(('node', 'rep'))
- feature_grad: bfloat16 [65536, 256], P(('node', 'rep'))
- weight_grad: float32 [256, 256], replicated
The draws below stay inside these ranges and needn't reach their ends.
Inputs may be any that keep to these rules, and one draw needn't show every extreme that they name: `tile_count`: slots at and beyond a device's count are ignored; some device has all 160 slots live in every draw.
All inputs are finite; a program needn't handle non-finite values.
Results may differ from the reference program's by a relative error of at most 0.007.
Values may be sent and summed in bfloat16 or wider, within the bound.
No kernel may reach another device: no remote copies, remote signals or barrier semaphores. Data moves between devices by JAX's collectives and lax.ppermute only.
A program may use at most 256 MiB of HBM per device.

```python
import jax
import jax.numpy as jnp
from jax import lax

BLOCK = 256
FEAT = 256
RB_DEV = 8
TILES_DEV = 160
NODES = 65536
COLS_REP = 64
N_NODE = 32
N_REP = 4


def draw_tile_count(key, part):
    base = jax.random.randint(key, (N_NODE * N_REP,), TILES_DEV // 2, TILES_DEV + 1)
    chosen = jax.random.randint(jax.random.fold_in(key, 7), (), 0, N_NODE * N_REP)
    places = jnp.arange(N_NODE * N_REP, dtype=jnp.int32)
    filled = jnp.where(places == chosen, TILES_DEV, base)
    return filled.reshape(N_NODE, N_REP).astype(jnp.int32)


def touch_ends(values, key, smallest, high):
    index_at = [jax.random.randint(jax.random.fold_in(key, axis), (), 0, length) for axis, length in enumerate(values.shape)]
    widest = values.shape.index(max(values.shape))
    beside = index_at[:widest] + [(index_at[widest] + 1) % values.shape[widest]] + index_at[widest + 1:]
    return values.at[tuple(index_at)].set(smallest).at[tuple(beside)].set(high)


def levels(rng, dims, split, least, largest):
    factor_of = 1.0
    for position, parts in split:
        draws = jax.random.uniform(jax.random.fold_in(jax.random.fold_in(rng, 6), position), (parts,), jnp.float32, least / len(split), largest / len(split))
        factor_of = factor_of * jnp.repeat(jnp.exp(draws), dims[position] // parts).reshape((-1,) + (1,) * (len(dims) - 1 - position))
    return factor_of


def bell_draw(stream_key, extent, deviation, reach, shards=(), kind=jnp.bfloat16):
    drawn = deviation * jax.random.normal(stream_key, extent, jnp.float32)
    if shards:
        drawn = drawn * levels(stream_key, extent, shards, -0.22, 0.18)
    return jnp.clip(drawn, -reach, reach).astype(kind)


def setup_inputs(seed: int = 0) -> dict:
    splits = jax.random.split(jax.random.key(seed), 8)
    return {
        "node_feats": bell_draw(splits[0], (NODES, FEAT), 1.0, 6.0, ((0, 32),)),
        "weight": bell_draw(splits[1], (FEAT, FEAT), FEAT ** -0.5, 0.375),
        "cotangent": bell_draw(splits[2], (NODES, FEAT), 1.0, 6.0, ((0, 128),)),
        "tiles": bell_draw(splits[3], (N_NODE, N_REP, TILES_DEV, BLOCK, BLOCK), 0.008, 0.049804688, ((0, 32), (1, 4))),
        "tile_rows": touch_ends(jax.random.randint(splits[4], (N_NODE, N_REP, TILES_DEV), 0, RB_DEV), jax.random.fold_in(splits[4], 1), 0, RB_DEV - 1).astype(jnp.int32),
        "tile_cols": touch_ends(jax.random.randint(splits[5], (N_NODE, N_REP, TILES_DEV), 0, COLS_REP), jax.random.fold_in(splits[5], 1), 0, COLS_REP - 1).astype(jnp.int32),
        "tile_count": draw_tile_count(jax.random.fold_in(splits[7], 71), 0),
    }


def reference(node_feats, weight, cotangent, tiles, tile_rows, tile_cols, tile_count):
    quarter = RB_DEV // N_REP
    blocks = NODES // BLOCK
    total_dev = N_NODE * N_REP
    flat_tiles = tiles.reshape(total_dev, TILES_DEV, BLOCK, BLOCK)
    flat_rows = tile_rows.reshape(total_dev, TILES_DEV)
    flat_cols = tile_cols.reshape(total_dev, TILES_DEV)
    flat_count = tile_count.reshape(total_dev)
    feat_blocks = node_feats.reshape(blocks, BLOCK, FEAT)
    slots = jnp.arange(TILES_DEV, dtype=jnp.int32)

    def places(device):
        node_idx = (device // N_REP).astype(jnp.int32)
        rep_idx = (device % N_REP).astype(jnp.int32)
        grow = node_idx * RB_DEV + flat_rows[device]
        comp = flat_cols[device]
        gcol = (comp // quarter) * RB_DEV + rep_idx * quarter + comp % quarter
        live = (slots < flat_count[device]).astype(jnp.float32)
        return grow.astype(jnp.int32), gcol.astype(jnp.int32), live

    def forward(device, acc):
        grow, gcol, live = places(device)
        tl = flat_tiles[device].astype(jnp.float32)
        src = feat_blocks[gcol].astype(jnp.float32)
        prod = jnp.einsum('tab,tbf->taf', tl, src) * live[:, None, None]
        return acc.at[grow].add(prod)

    agg = lax.fori_loop(0, total_dev, forward, jnp.zeros((blocks, BLOCK, FEAT), jnp.float32))
    aggregated = agg.reshape(NODES, FEAT).astype(jnp.bfloat16)
    pre = jnp.dot(aggregated, weight, preferred_element_type=jnp.float32)
    sig = jax.nn.sigmoid(pre)
    activated = (pre * sig).astype(jnp.bfloat16)
    dpre = (cotangent.astype(jnp.float32) * sig * (1.0 + pre * (1.0 - sig))).astype(jnp.bfloat16)
    weight_grad = jnp.dot(aggregated.T, dpre, preferred_element_type=jnp.float32) * (float(NODES) ** -0.5)
    dagg = jnp.dot(dpre, weight.T, preferred_element_type=jnp.float32).astype(jnp.bfloat16)
    dagg_blocks = dagg.reshape(blocks, BLOCK, FEAT)

    def backward(device, acc):
        grow, gcol, live = places(device)
        tl = flat_tiles[device].astype(jnp.float32)
        src = dagg_blocks[grow].astype(jnp.float32)
        prod = jnp.einsum('tab,taf->tbf', tl, src) * live[:, None, None]
        return acc.at[gcol].add(prod)

    grads = lax.fori_loop(0, total_dev, backward, jnp.zeros((blocks, BLOCK, FEAT), jnp.float32))
    feature_grad = grads.reshape(NODES, FEAT).astype(jnp.bfloat16)
    return activated, feature_grad, weight_grad
```

```python
import functools

import jax
import jax.numpy as jnp
from jax import lax
from jax.experimental import pallas as pl
from jax.experimental.pallas import tpu as pltpu
from jax.sharding import PartitionSpec as P

AXES = ("node", "rep")
NZ, NYL, NX, NYH, NC = 4, 2, 4, 2, 2
B = 256
F32, BF16, I32 = jnp.float32, jnp.bfloat16, jnp.int32
NBUF = 8
MIB = 1 << 20


def _flat(z, yl, x, yh, c):
    return ((((z % NZ) * NYL + yl) * NX + x % NX) * NYH + yh) * NC + c


def _perm(dz=0, dyl=0, dx=0, dyh=0, dc=0):
    pairs = []
    for z in range(NZ):
        for yl in range(NYL):
            for x in range(NX):
                for yh in range(NYH):
                    for c in range(NC):
                        pairs.append(
                            (
                                _flat(z, yl, x, yh, c),
                                _flat(z + dz, yl ^ dyl, x + dx, yh ^ dyh, c ^ dc),
                            )
                        )
    return pairs


XP, XM, ZP, ZM = _perm(dx=1), _perm(dx=-1), _perm(dz=1), _perm(dz=-1)
YN, YH, CC = _perm(dyl=1), _perm(dyh=1), _perm(dc=1)


def send(value, pairs):
    return lax.ppermute(value, AXES, pairs)


def _sorted(v):
    n = v.shape[0]
    rank = jnp.sum((v[None, :] < v[:, None]).astype(I32), axis=1)
    hit = rank[:, None] == jnp.arange(n, dtype=I32)[None, :]
    return jnp.sum(jnp.where(hit, v[:, None], 0), axis=0)


def tables(rows, cols, count, z, yl, x, yh, c):
    slots = jnp.arange(rows.shape[0], dtype=I32)
    j = cols % 2
    xr = (cols // 2 % NX - x) % NX
    yr = (cols // (2 * NX) % NYL) ^ yl
    zr = (cols // (2 * NX * NYL) - z) % NZ
    near = lambda r: jnp.where(r == 0, 0, jnp.where(r == 3, 1, jnp.where(r == 1, 2, 3)))
    outer = jnp.where(j == 0, zr, xr)
    inner = jnp.where(j == 0, xr, zr)
    chunk = jnp.where(outer == 0, 0, jnp.where(outer == 2, 2, 1))
    place = near(inner) * 2 + yr
    wide = j * 16 + jnp.where(outer == 3, 0, 8) + place
    fidx = jnp.where(chunk == 1, wide, j * 8 + place)
    q = rows // 2
    rpos = ((q % 2) ^ c) * 4 + ((q // 2) ^ yh) * 2 + rows % 2
    chunk = jnp.where(slots < count, chunk, 3)
    fwd = _sorted((chunk << 24) | (rpos << 18) | (fidx << 8) | slots)
    bwd = _sorted((chunk << 24) | (fidx << 18) | (rpos << 8) | slots)
    offs = jnp.sum((chunk[None, :] < jnp.arange(4, dtype=I32)[:, None]).astype(I32), axis=1)
    return fwd, bwd, offs


def _tile_loop(tab, first, count, tiles, tbuf, tsem, step, unroll):
    def fetch(i):
        slot = tab[first + i] & 255
        at = lax.rem(i, NBUF)
        return pltpu.make_async_copy(tiles.at[slot], tbuf.at[at], tsem.at[at])

    def prime(i, carry):
        fetch(i).start()
        return carry

    def run(base, width):
        for u in range(width):
            fetch(base + u).wait()
        for u in range(width):
            i = base + u
            step(tab[first + i], tbuf.at[lax.rem(i, NBUF)])
        for u in range(width):
            i = base + u

            @pl.when(i + NBUF < count)
            def _():
                fetch(i + NBUF).start()

    whole = count // unroll

    def body():
        def many(g, carry):
            run(g * unroll, unroll)
            return carry

        def one(i, carry):
            run(i, 1)
            return carry

        lax.fori_loop(0, whole, many, 0)
        lax.fori_loop(whole * unroll, count, one, 0)

    return lambda: lax.fori_loop(0, jnp.minimum(count, NBUF), prime, 0), body


def _forward_kernel(chunk, nbuf, last, tab, offs, tiles, *refs):
    bufs, refs = refs[:nbuf], refs[nbuf:]
    if chunk:
        acc_in, refs = refs[0], refs[1:]
    outs, (feats, acc, tbuf, tsem, fsem, asem) = refs[:-6], refs[-6:]
    first = offs[chunk]
    count = offs[chunk + 1] - first

    def step(word, tile):
        r = (word >> 18) & 7
        f = (word >> 8) & 31
        acc[r] += jnp.dot(tile[...], feats[f], preferred_element_type=F32)

    prime, body = _tile_loop(tab, first, count, tiles, tbuf, tsem, step, 2)
    prime()
    copies = []
    at = 0
    for k, b in enumerate(bufs):
        n = b.shape[0]
        copies.append(pltpu.make_async_copy(b, feats.at[pl.ds(at, n)], fsem.at[k]))
        at += n
    if chunk:
        copies.append(pltpu.make_async_copy(acc_in, acc, asem))
    for cp in copies:
        cp.start()
    if not chunk:
        acc[...] = jnp.zeros_like(acc)
    for cp in copies:
        cp.wait()
    body()
    if last:
        half = acc.shape[0] // 2
        outcp = [
            pltpu.make_async_copy(acc.at[pl.ds(0, half)], outs[0], fsem.at[0]),
            pltpu.make_async_copy(acc.at[pl.ds(half, half)], outs[1], fsem.at[1]),
        ]
    else:
        outcp = [pltpu.make_async_copy(acc, outs[0], asem)]
    for cp in outcp:
        cp.start()
    for cp in outcp:
        cp.wait()


ANY = pl.BlockSpec(memory_space=pl.ANY)
SMEM = pl.BlockSpec(memory_space=pltpu.SMEM)
VMEM = pl.BlockSpec(memory_space=pltpu.VMEM)


def forward(chunk, tab, offs, tiles, bufs, acc, share):
    nblk = sum(b.shape[0] for b in bufs)
    last = chunk == 2
    full = jax.ShapeDtypeStruct((8, B, B), F32)
    half = jax.ShapeDtypeStruct((4, B, B), F32)
    outs = [half, half] if last else [full]
    args = [tab, offs, tiles, *bufs] + ([acc] if chunk else [])
    work = int(160 * share)
    res = pl.pallas_call(
        functools.partial(_forward_kernel, chunk, len(bufs), last),
        name=f"tiles_forward_{chunk}",
        in_specs=[SMEM, SMEM] + [ANY] * (len(args) - 2),
        out_specs=[ANY] * len(outs),
        out_shape=outs,
        scratch_shapes=[
            pltpu.VMEM((nblk, B, B), BF16),
            pltpu.VMEM((8, B, B), F32),
            pltpu.VMEM((NBUF, B, B), BF16),
            pltpu.SemaphoreType.DMA((NBUF,)),
            pltpu.SemaphoreType.DMA((max(2, len(bufs)),)),
            pltpu.SemaphoreType.DMA,
        ],
        compiler_params=pltpu.CompilerParams(vmem_limit_bytes=16 * MIB),
        cost_estimate=pl.CostEstimate(
            flops=work * 2 * B**3, bytes_accessed=work * B * B * 2 + 6 * MIB, transcendentals=0
        ),
    )(*args)
    return res if last else res[0]


def _backward_kernel(chunk, nout, tab, offs, tiles, d0, d1, *refs):
    outs, (dagg, acc, stage, tbuf, tsem, dsem, osem) = refs[:nout], refs[nout:]
    first = offs[chunk]
    count = offs[chunk + 1] - first

    def step(word, tile):
        f = (word >> 18) & 31
        r = (word >> 8) & 7
        acc[f] += jnp.dot(dagg[r], tile[...], preferred_element_type=F32)

    prime, body = _tile_loop(tab, first, count, tiles, tbuf, tsem, step, 2)
    prime()
    copies = [
        pltpu.make_async_copy(d0, dagg.at[pl.ds(0, 4)], dsem.at[0]),
        pltpu.make_async_copy(d1, dagg.at[pl.ds(4, 4)], dsem.at[1]),
    ]
    for cp in copies:
        cp.start()
    acc[...] = jnp.zeros_like(acc)
    for cp in copies:
        cp.wait()
    body()
    at = 0
    writes = []
    for k, o in enumerate(outs):
        n = o.shape[0]
        for m in range(n):
            stage[at + m] = acc[at + m].astype(BF16)
        cp = pltpu.make_async_copy(stage.at[pl.ds(at, n)], o, osem.at[k])
        cp.start()
        writes.append(cp)
        at += n
    for cp in writes:
        cp.wait()


def backward(chunk, tab, offs, tiles, d0, d1, sizes, share):
    nblk = sum(sizes)
    work = int(160 * share)
    return pl.pallas_call(
        functools.partial(_backward_kernel, chunk, len(sizes)),
        name=f"tiles_backward_{chunk}",
        in_specs=[SMEM, SMEM] + [ANY] * 3,
        out_specs=[ANY] * len(sizes),
        out_shape=[jax.ShapeDtypeStruct((n, B, B), BF16) for n in sizes],
        scratch_shapes=[
            pltpu.VMEM((8, B, B), BF16),
            pltpu.VMEM((nblk, B, B), F32),
            pltpu.VMEM((nblk, B, B), BF16),
            pltpu.VMEM((NBUF, B, B), BF16),
            pltpu.SemaphoreType.DMA((NBUF,)),
            pltpu.SemaphoreType.DMA((2,)),
            pltpu.SemaphoreType.DMA((len(sizes),)),
        ],
        compiler_params=pltpu.CompilerParams(vmem_limit_bytes=24 * MIB),
        cost_estimate=pl.CostEstimate(
            flops=work * 2 * B**3, bytes_accessed=work * B * B * 2 + 6 * MIB, transcendentals=0
        ),
    )(tab, offs, tiles, d0, d1)


def _dense_kernel(mine, core, far, cot0, cot1, w_ref, act, dagg, wterm):
    w = w_ref[...]
    for k in range(4):
        agg = (mine[k] + core[k] + far[(k + 2) % 4].astype(F32)).astype(BF16)
        pre = jnp.dot(agg, w, preferred_element_type=F32)
        sig = jax.nn.sigmoid(pre)
        cot = (cot0 if k < 2 else cot1)[k % 2].astype(F32)
        dpre = (cot * sig * (1.0 + pre * (1.0 - sig))).astype(BF16)
        dagg[k] = lax.dot_general(
            w, dpre, (((1,), (1,)), ((), ())), preferred_element_type=F32
        ).astype(BF16)
        if k < 2:
            act[k] = (pre * sig).astype(BF16)
            term = lax.dot_general(
                agg, dpre, (((0,), (0,)), ((), ())), preferred_element_type=F32
            )
            wterm[...] = term if k == 0 else wterm[...] + term


def dense(mine, core, far, cot0, cot1, w):
    return pl.pallas_call(
        _dense_kernel,
        name="dense",
        in_specs=[VMEM] * 6,
        out_specs=[VMEM] * 3,
        out_shape=[
            jax.ShapeDtypeStruct((2, B, B), BF16),
            jax.ShapeDtypeStruct((4, B, B), BF16),
            jax.ShapeDtypeStruct((B, B), F32),
        ],
        compiler_params=pltpu.CompilerParams(vmem_limit_bytes=16 * MIB),
        cost_estimate=pl.CostEstimate(
            flops=10 * 2 * B**3, bytes_accessed=5 * MIB, transcendentals=1024 * 256
        ),
    )(mine, core, far, cot0, cot1, w)


def plus(*terms):
    total = terms[0].astype(F32)
    for t in terms[1:]:
        total = total + t.astype(F32)
    return total.astype(BF16)


def gather(own):
    other = send(own, YN)
    e0 = jnp.stack([own[0], other[0]])
    o0 = jnp.stack([own[1], other[1]])
    e_m, e_p = send(e0, XP), send(e0, XM)
    o_m, o_p = send(o0, ZP), send(o0, ZM)
    e_a, e_b = send(e_m[:1], XP), send(e_p[1:], XM)
    o_a, o_b = send(o_m[:1], ZP), send(o_p[1:], ZM)
    even = jnp.concatenate([e0, e_m, e_p, e_a, e_b])
    odd = jnp.concatenate([o0, o_m, o_p, o_a, o_b])
    em, ep = send(even, ZP), send(even, ZM)
    om, op = send(odd, XP), send(odd, XM)
    ea, eb = send(em[:4], ZP), send(ep[4:], ZM)
    oa, ob = send(om[:4], XP), send(op[4:], XM)
    return [even, odd], [em, ep, om, op], [ea, eb, oa, ob]


def body(node_feats, weight, cotangent, tiles, tile_rows, tile_cols, tile_count):
    node, rep = lax.axis_index("node"), lax.axis_index("rep")
    x, yl, z = node % NX, node // NX % NYL, node // (NX * NYL)
    c, yh = rep % NC, rep // NC
    tiles = tiles[0, 0]
    fwd, bwd, offs = tables(
        tile_rows[0, 0], tile_cols[0, 0], tile_count[0, 0], z, yl, x, yh, c
    )
    own = lax.dynamic_slice_in_dim(node_feats.reshape(8, B, B), rep * 2, 2, 0)
    cot0 = cotangent.reshape(2, B, B)
    cot1 = send(cot0, YH)
    near, mid, far = gather(own)
    acc = forward(0, fwd, offs, tiles, near, None, 0.25)
    acc = forward(1, fwd, offs, tiles, mid, acc, 0.5)
    mine, theirs = forward(2, fwd, offs, tiles, far, acc, 0.25)
    core = send(theirs, CC)
    across = send((mine + core).astype(BF16), YH)
    act, d0, term = dense(mine, core, across, cot0, cot1, weight)
    d1 = send(d0, CC)
    scale = float(node_feats.shape[0] * NZ * NYL * NX) ** (-0.5)
    weight_grad = lax.psum(term, AXES) * scale

    ea, eb, oa, ob = backward(2, bwd, offs, tiles, d0, d1, [4, 4, 4, 4], 0.25)
    ra, rb = send(ea, ZP), send(eb, ZM)
    sa, sb = send(oa, XP), send(ob, XM)
    em0, em1, ep0, ep1, om0, om1, op0, op1 = backward(
        1, bwd, offs, tiles, d0, d1, [4] * 8, 0.5
    )
    even, odd = backward(0, bwd, offs, tiles, d0, d1, [8, 8], 0.25)
    to_zp = jnp.concatenate([plus(ep0, ra), ep1])
    to_zm = jnp.concatenate([em0, plus(em1, rb)])
    to_xp = jnp.concatenate([plus(op0, sa), op1])
    to_xm = jnp.concatenate([om0, plus(om1, sb)])
    even = plus(even, send(to_zp, ZP), send(to_zm, ZM))
    odd = plus(odd, send(to_xp, XP), send(to_xm, XM))

    def inner(q, up, down):
        ca, cb = send(q[6:7], up), send(q[7:8], down)
        to_up = jnp.concatenate([plus(q[4:5], ca), q[5:6]])
        to_down = jnp.concatenate([q[2:3], plus(q[3:4], cb)])
        return q[0:2], send(to_up, up), send(to_down, down)

    ge = inner(even, XP, XM)
    go = inner(odd, ZP, ZM)
    ge = plus(*ge)
    go = plus(*go)
    other = send(jnp.stack([ge[1], go[1]]), YN)
    total = jnp.stack([ge[0], go[0]]).astype(F32) + other.astype(F32)
    feature_grad = jnp.swapaxes(total, 1, 2).astype(BF16).reshape(2 * B, B)
    return act.reshape(2 * B, B), feature_grad, weight_grad


def solution(mesh):
    placed = (
        P("node", None),
        P(),
        P(("node", "rep"), None),
        P("node", "rep", None, None, None),
        P("node", "rep", None),
        P("node", "rep", None),
        P("node", "rep"),
    )
    return jax.shard_map(
        body,
        mesh=mesh,
        in_specs=placed,
        out_specs=(P(("node", "rep"), None), P(("node", "rep"), None), P()),
        check_vma=False,
    )
```

```python
import functools

import jax
import jax.numpy as jnp
from jax import lax
from jax.experimental import pallas as pl
from jax.experimental.pallas import tpu as pltpu
from jax.sharding import PartitionSpec as P

AXES = ("node", "rep")
NZ, NYL, NX, NYH, NC = 4, 2, 4, 2, 2
B = 256
F32, BF16, I32 = jnp.float32, jnp.bfloat16, jnp.int32
NBUF = 32
UNROLL = 8
MIB = 1 << 20


def _flat(z, yl, x, yh, c):
    return ((((z % NZ) * NYL + yl) * NX + x % NX) * NYH + yh) * NC + c


def _perm(dz=0, dyl=0, dx=0, dyh=0, dc=0):
    pairs = []
    for z in range(NZ):
        for yl in range(NYL):
            for x in range(NX):
                for yh in range(NYH):
                    for c in range(NC):
                        pairs.append(
                            (
                                _flat(z, yl, x, yh, c),
                                _flat(z + dz, yl ^ dyl, x + dx, yh ^ dyh, c ^ dc),
                            )
                        )
    return pairs


XP, XM, ZP, ZM = _perm(dx=1), _perm(dx=-1), _perm(dz=1), _perm(dz=-1)
X2, Z2 = _perm(dx=2), _perm(dz=2)
YN, YH, CC = _perm(dyl=1), _perm(dyh=1), _perm(dc=1)


def _pairs(axis, top):
    move = lambda k: top - k if top else k ^ 1
    out = []
    for z in range(NZ):
        for yl in range(NYL):
            for x in range(NX):
                for yh in range(NYH):
                    for c in range(NC):
                        to = (move(z), yl, x) if axis == "z" else (z, yl, move(x))
                        out.append((_flat(z, yl, x, yh, c), _flat(*to, yh, c)))
    return out


XE, XO, ZE, ZO = _pairs("x", 0), _pairs("x", 3), _pairs("z", 0), _pairs("z", 3)


def send(value, pairs):
    return lax.ppermute(value, AXES, pairs)


def tie(value, *deps):
    return lax.optimization_barrier((value, *deps))[0]


def _sorted(v):
    n = v.shape[0]
    rank = jnp.sum((v[None, :] < v[:, None]).astype(I32), axis=1)
    hit = rank[:, None] == jnp.arange(n, dtype=I32)[None, :]
    return jnp.sum(jnp.where(hit, v[:, None], 0), axis=0)


def tables(rows, cols, count, z, yl, x, yh, c):
    slots = jnp.arange(rows.shape[0], dtype=I32)
    j = cols % 2
    xr = (cols // 2 % NX - x) % NX
    yr = (cols // (2 * NX) % NYL) ^ yl
    zr = (cols // (2 * NX * NYL) - z) % NZ
    near = lambda r: jnp.where(r == 0, 0, jnp.where(r == 3, 1, jnp.where(r == 1, 2, 3)))
    outer = jnp.where(j == 0, zr, xr)
    inner = jnp.where(j == 0, xr, zr)
    chunk = jnp.where(outer == 0, 0, jnp.where(outer == 2, 2, 1))
    place = near(inner) * 2 + yr
    wide = j * 16 + jnp.where(outer == 3, 0, 8) + place
    fidx = jnp.where(chunk == 1, wide, j * 8 + place)
    q = rows // 2
    rpos = ((q % 2) ^ c) * 4 + ((q // 2) ^ yh) * 2 + rows % 2
    chunk = jnp.where(slots < count, chunk, 3)
    fwd = _sorted((chunk << 24) | (rpos << 18) | (fidx << 8) | slots)
    bwd = _sorted((chunk << 24) | (fidx << 18) | (rpos << 8) | slots)
    offs = jnp.sum((chunk[None, :] < jnp.arange(4, dtype=I32)[:, None]).astype(I32), axis=1)
    return fwd, bwd, offs


def _tile_loop(tab, first, count, tiles, tbuf, tsem, step, unroll):
    def fetch(i):
        slot = tab[first + i] & 255
        at = lax.rem(i, NBUF)
        return pltpu.make_async_copy(tiles.at[slot], tbuf.at[at], tsem.at[at])

    def prime(i, carry):
        fetch(i).start()
        return carry

    def run(base, width):
        for u in range(width):
            fetch(base + u).wait()
        for u in range(width):
            i = base + u
            step(tab[first + i], tbuf.at[lax.rem(i, NBUF)])
        for u in range(width):
            i = base + u

            @pl.when(i + NBUF < count)
            def _():
                fetch(i + NBUF).start()

    whole = count // unroll

    def body():
        def many(g, carry):
            run(g * unroll, unroll)
            return carry

        def one(i, carry):
            run(i, 1)
            return carry

        lax.fori_loop(0, whole, many, 0)
        lax.fori_loop(whole * unroll, count, one, 0)

    return lambda: lax.fori_loop(0, jnp.minimum(count, NBUF), prime, 0), body


def _forward_kernel(chunk, nbuf, last, tab, offs, tiles, *refs):
    bufs, refs = refs[:nbuf], refs[nbuf:]
    if chunk:
        acc_in, refs = refs[0], refs[1:]
    outs, (feats, acc, tbuf, tsem, fsem, asem) = refs[:-6], refs[-6:]
    first = offs[chunk]
    count = offs[chunk + 1] - first

    def step(word, tile):
        r = (word >> 18) & 7
        f = (word >> 8) & 31
        acc[r] += jnp.dot(tile[...], feats[f], preferred_element_type=F32)

    prime, body = _tile_loop(tab, first, count, tiles, tbuf, tsem, step, UNROLL)
    prime()
    copies = []
    at = 0
    for k, b in enumerate(bufs):
        n = b.shape[0]
        copies.append(pltpu.make_async_copy(b, feats.at[pl.ds(at, n)], fsem.at[k]))
        at += n
    if chunk:
        copies.append(pltpu.make_async_copy(acc_in, acc, asem))
    for cp in copies:
        cp.start()
    if not chunk:
        acc[...] = jnp.zeros_like(acc)
    for cp in copies:
        cp.wait()
    body()
    if last:
        half = acc.shape[0] // 2
        outcp = [
            pltpu.make_async_copy(acc.at[pl.ds(0, half)], outs[0], fsem.at[0]),
            pltpu.make_async_copy(acc.at[pl.ds(half, half)], outs[1], fsem.at[1]),
        ]
    else:
        outcp = [pltpu.make_async_copy(acc, outs[0], asem)]
    for cp in outcp:
        cp.start()
    for cp in outcp:
        cp.wait()


ANY = pl.BlockSpec(memory_space=pl.ANY)
SMEM = pl.BlockSpec(memory_space=pltpu.SMEM)
VMEM = pl.BlockSpec(memory_space=pltpu.VMEM)


def forward(chunk, tab, offs, tiles, bufs, acc, share):
    nblk = sum(b.shape[0] for b in bufs)
    last = chunk == 2
    full = jax.ShapeDtypeStruct((8, B, B), F32)
    half = jax.ShapeDtypeStruct((4, B, B), F32)
    outs = [half, half] if last else [full]
    args = [tab, offs, tiles, *bufs] + ([acc] if chunk else [])
    work = int(160 * share)
    res = pl.pallas_call(
        functools.partial(_forward_kernel, chunk, len(bufs), last),
        name=f"tiles_forward_{chunk}",
        in_specs=[SMEM, SMEM] + [ANY] * (len(args) - 2),
        out_specs=[ANY] * len(outs),
        out_shape=outs,
        scratch_shapes=[
            pltpu.VMEM((nblk, B, B), BF16),
            pltpu.VMEM((8, B, B), F32),
            pltpu.VMEM((NBUF, B, B), BF16),
            pltpu.SemaphoreType.DMA((NBUF,)),
            pltpu.SemaphoreType.DMA((max(2, len(bufs)),)),
            pltpu.SemaphoreType.DMA,
        ],
        compiler_params=pltpu.CompilerParams(vmem_limit_bytes=16 * MIB),
        cost_estimate=pl.CostEstimate(
            flops=work * 2 * B**3, bytes_accessed=work * B * B * 2 + 6 * MIB, transcendentals=0
        ),
    )(*args)
    return res if last else res[0]


def _backward_kernel(chunk, nout, tab, offs, tiles, d0, d1, *refs):
    outs, (dagg, acc, stage, tbuf, tsem, dsem, osem) = refs[:nout], refs[nout:]
    first = offs[chunk]
    count = offs[chunk + 1] - first

    def step(word, tile):
        f = (word >> 18) & 31
        r = (word >> 8) & 7
        acc[f] += jnp.dot(dagg[r], tile[...], preferred_element_type=F32)

    prime, body = _tile_loop(tab, first, count, tiles, tbuf, tsem, step, UNROLL)
    prime()
    copies = [
        pltpu.make_async_copy(d0, dagg.at[pl.ds(0, 4)], dsem.at[0]),
        pltpu.make_async_copy(d1, dagg.at[pl.ds(4, 4)], dsem.at[1]),
    ]
    for cp in copies:
        cp.start()
    acc[...] = jnp.zeros_like(acc)
    for cp in copies:
        cp.wait()
    body()
    at = 0
    writes = []
    for k, o in enumerate(outs):
        n = o.shape[0]
        for m in range(n):
            stage[at + m] = acc[at + m].astype(BF16)
        cp = pltpu.make_async_copy(stage.at[pl.ds(at, n)], o, osem.at[k])
        cp.start()
        writes.append(cp)
        at += n
    for cp in writes:
        cp.wait()


def backward(chunk, tab, offs, tiles, d0, d1, sizes, share):
    nblk = sum(sizes)
    work = int(160 * share)
    return pl.pallas_call(
        functools.partial(_backward_kernel, chunk, len(sizes)),
        name=f"tiles_backward_{chunk}",
        in_specs=[SMEM, SMEM] + [ANY] * 3,
        out_specs=[ANY] * len(sizes),
        out_shape=[jax.ShapeDtypeStruct((n, B, B), BF16) for n in sizes],
        scratch_shapes=[
            pltpu.VMEM((8, B, B), BF16),
            pltpu.VMEM((nblk, B, B), F32),
            pltpu.VMEM((nblk, B, B), BF16),
            pltpu.VMEM((NBUF, B, B), BF16),
            pltpu.SemaphoreType.DMA((NBUF,)),
            pltpu.SemaphoreType.DMA((2,)),
            pltpu.SemaphoreType.DMA((len(sizes),)),
        ],
        compiler_params=pltpu.CompilerParams(vmem_limit_bytes=24 * MIB),
        cost_estimate=pl.CostEstimate(
            flops=work * 2 * B**3, bytes_accessed=work * B * B * 2 + 6 * MIB, transcendentals=0
        ),
    )(tab, offs, tiles, d0, d1)


def _dense_kernel(near, far, cot0, cot1, w_ref, act, dagg, wterm):
    w = w_ref[...]
    for k in range(4):
        agg = (near[k].astype(F32) + far[(k + 2) % 4].astype(F32)).astype(BF16)
        pre = jnp.dot(agg, w, preferred_element_type=F32)
        sig = jax.nn.sigmoid(pre)
        cot = (cot0 if k < 2 else cot1)[k % 2].astype(F32)
        dpre = (cot * sig * (1.0 + pre * (1.0 - sig))).astype(BF16)
        dagg[k] = lax.dot_general(
            w, dpre, (((1,), (1,)), ((), ())), preferred_element_type=F32
        ).astype(BF16)
        term = lax.dot_general(agg, dpre, (((0,), (0,)), ((), ())), preferred_element_type=F32)
        if k < 2:
            act[k] = (pre * sig).astype(BF16)
        if k % 2 == 0:
            wterm[k // 2] = term
        else:
            wterm[k // 2] = wterm[k // 2] + term


def dense(near, far, cot0, cot1, w):
    return pl.pallas_call(
        _dense_kernel,
        name="dense",
        in_specs=[VMEM] * 5,
        out_specs=[VMEM] * 3,
        out_shape=[
            jax.ShapeDtypeStruct((2, B, B), BF16),
            jax.ShapeDtypeStruct((4, B, B), BF16),
            jax.ShapeDtypeStruct((2, B, B), F32),
        ],
        compiler_params=pltpu.CompilerParams(vmem_limit_bytes=16 * MIB),
        cost_estimate=pl.CostEstimate(
            flops=10 * 2 * B**3, bytes_accessed=5 * MIB, transcendentals=1024 * 256
        ),
    )(near, far, cot0, cot1, w)


def plus(*terms):
    total = terms[0].astype(F32)
    for t in terms[1:]:
        total = total + t.astype(F32)
    return total.astype(BF16)


def weight_sum(term, c, yh):
    a, b = term[0], term[1]
    half = B // 2
    whole = a + b
    keep = lax.dynamic_slice_in_dim(whole, c * half, half, 0)
    give = lax.dynamic_slice_in_dim(whole, (1 - c) * half, half, 0)
    keep = keep + send(give, CC)
    for pairs in (YN, XE, ZE, XO, ZO):
        keep = keep + send(keep, pairs)
    got = send(keep, CC)
    return jnp.where(c == 0, jnp.concatenate([keep, got]), jnp.concatenate([got, keep]))


def body(node_feats, weight, cotangent, tiles, tile_rows, tile_cols, tile_count):
    node, rep = lax.axis_index("node"), lax.axis_index("rep")
    x, yl, z = node % NX, node // NX % NYL, node // (NX * NYL)
    c, yh = rep % NC, rep // NC
    tiles = pltpu.with_memory_space_constraint(tiles[0, 0], pltpu.HBM)
    fwd, bwd, offs = tables(
        tile_rows[0, 0], tile_cols[0, 0], tile_count[0, 0], z, yl, x, yh, c
    )
    own = lax.dynamic_slice_in_dim(node_feats.reshape(8, B, B), rep * 2, 2, 0)
    cot0 = cotangent.reshape(2, B, B)

    other = send(own, YN)
    e0 = jnp.stack([own[0], other[0]])
    o0 = jnp.stack([own[1], other[1]])
    e_m, e_p, e_2 = send(e0, XP), send(e0, XM), send(e0, X2)
    o_m, o_p, o_2 = send(o0, ZP), send(o0, ZM), send(o0, Z2)
    even = jnp.concatenate([e0, e_m, e_p, e_2])
    odd = jnp.concatenate([o0, o_m, o_p, o_2])
    cot1 = send(tie(cot0, even, odd), YH)
    em, ep = send(even, ZP), send(even, ZM)
    om, op = send(odd, XP), send(odd, XM)
    acc = forward(0, fwd, offs, tiles, [even, odd], None, 0.25)
    em, ep, om, op, acc, cot1 = lax.optimization_barrier((em, ep, om, op, acc, cot1))
    ea, eb = send(em[:4], ZP), send(ep[4:], ZM)
    oa, ob = send(om[:4], XP), send(op[4:], XM)
    acc = forward(1, fwd, offs, tiles, [em, ep, om, op], acc, 0.5)
    mine, theirs = forward(2, fwd, offs, tiles, [ea, eb, oa, ob], acc, 0.25)
    core = send(theirs, CC)
    part = (mine + core).astype(BF16)
    across = send(part, YH)
    act, d0, term = dense(part, across, cot0, cot1, weight)
    d1 = send(d0, CC)

    ea, eb, oa, ob = backward(2, bwd, offs, tiles, d0, d1, [4, 4, 4, 4], 0.25)
    ra, rb = send(ea, ZP), send(eb, ZM)
    sa, sb = send(oa, XP), send(ob, XM)
    d0, d1, ea, eb, oa, ob = lax.optimization_barrier((d0, d1, ea, eb, oa, ob))
    em, ep, om, op = backward(1, bwd, offs, tiles, d0, d1, [8] * 4, 0.5)
    even, odd = backward(0, bwd, offs, tiles, d0, d1, [8, 8], 0.25)
    em, ep, om, op, even, odd, ra, rb, sa, sb = lax.optimization_barrier(
        (em, ep, om, op, even, odd, ra, rb, sa, sb)
    )
    ep = ep.at[:4].set(plus(ep[:4], ra))
    em = em.at[4:].set(plus(em[4:], rb))
    op = op.at[:4].set(plus(op[:4], sa))
    om = om.at[4:].set(plus(om[4:], sb))
    even = plus(even, send(ep, ZP), send(em, ZM))
    odd = plus(odd, send(op, XP), send(om, XM))
    ge = plus(even[0:2], send(even[4:6], XP), send(even[2:4], XM), send(even[6:8], X2))
    go = plus(odd[0:2], send(odd[4:6], ZP), send(odd[2:4], ZM), send(odd[6:8], Z2))
    other = send(jnp.stack([ge[1], go[1]]), YN)
    total = jnp.stack([ge[0], go[0]]).astype(F32) + other.astype(F32)
    feature_grad = jnp.swapaxes(total, 1, 2).astype(BF16).reshape(2 * B, B)
    scale = float(node_feats.shape[0] * NZ * NYL * NX) ** (-0.5)
    weight_grad = weight_sum(term, c, yh) * scale
    return act.reshape(2 * B, B), feature_grad, weight_grad


def solution(mesh):
    placed = (
        P("node", None),
        P(),
        P(("node", "rep"), None),
        P("node", "rep", None, None, None),
        P("node", "rep", None),
        P("node", "rep", None),
        P("node", "rep"),
    )
    return jax.shard_map(
        body,
        mesh=mesh,
        in_specs=placed,
        out_specs=(P(("node", "rep"), None), P(("node", "rep"), None), P()),
        check_vma=False,
    )
```

```python
import functools

import jax
import jax.numpy as jnp
from jax import lax
from jax.experimental import pallas as pl
from jax.experimental.pallas import tpu as pltpu
from jax.sharding import PartitionSpec as P

AXES = ("node", "rep")
NZ, NYL, NX, NYH, NC = 4, 2, 4, 2, 2
B = 256
F32, BF16, I32 = jnp.float32, jnp.bfloat16, jnp.int32
NBUF = 32
UNROLL = 4
MIB = 1 << 20


def _flat(z, yl, x, yh, c):
    return ((((z % NZ) * NYL + yl) * NX + x % NX) * NYH + yh) * NC + c


def _perm(move):
    pairs = []
    for z in range(NZ):
        for yl in range(NYL):
            for x in range(NX):
                for yh in range(NYH):
                    for c in range(NC):
                        pairs.append((_flat(z, yl, x, yh, c), _flat(*move(z, yl, x, yh, c))))
    return pairs


def _along(first, step):
    def move(z, yl, x, yh, c):
        if (c == 0) == first:
            return z, yl, step(x), yh, c
        return step(z), yl, x, yh, c

    return _perm(move)


UP, UM, U2 = (_along(True, lambda k, d=d: k + d) for d in (1, -1, 2))
VP, VM, V2 = (_along(False, lambda k, d=d: k + d) for d in (1, -1, 2))
YN = _perm(lambda z, yl, x, yh, c: (z, 1 - yl, x, yh, c))
YH = _perm(lambda z, yl, x, yh, c: (z, yl, x, 1 - yh, c))
CC = _perm(lambda z, yl, x, yh, c: (z, yl, x, yh, 1 - c))


def send(value, pairs):
    return lax.ppermute(value, AXES, pairs)


def tie(value, *deps):
    return lax.optimization_barrier((value, *deps))[0]


def _sorted(v):
    n = v.shape[0]
    rank = jnp.sum((v[None, :] < v[:, None]).astype(I32), axis=1)
    hit = rank[:, None] == jnp.arange(n, dtype=I32)[None, :]
    return jnp.sum(jnp.where(hit, v[:, None], 0), axis=0)


def tables(rows, cols, count, z, yl, x, yh, c):
    slots = jnp.arange(rows.shape[0], dtype=I32)
    live = slots < count
    j = cols % 2
    xr = (cols // 2 % NX - x) % NX
    yr = (cols // (2 * NX) % NYL) ^ yl
    zr = (cols // (2 * NX * NYL) - z) % NZ
    ur = jnp.where(c == 0, xr, zr)
    vr = jnp.where(c == 0, zr, xr)
    at = jnp.where(ur == 0, 0, jnp.where(ur == 3, 1, jnp.where(ur == 1, 2, 3)))
    block = at * 4 + yr * 2 + j
    h = block // 8
    far = jnp.where(vr == 2, 6 + h, jnp.where(vr == 3, 2 + 2 * h, h))
    seg = jnp.where(vr == 1, 3 + 2 * h, far)
    bseg = jnp.where(vr == 1, 5 - 2 * h, far)
    q = rows // 2
    rpos = ((q % 2) ^ c) * 4 + ((q // 2) ^ yh) * 2 + rows % 2
    ends = jnp.arange(9, dtype=I32)[:, None]

    def offsets(key):
        return jnp.sum((key[None, :] < ends).astype(I32), axis=1)

    fkey = jnp.where(live, seg, 8)
    bkey = jnp.where(live, (bseg // 2) * 2 + rpos // 4, 8)
    col = (bseg % 2) * 8 + block % 8
    fwd = _sorted((fkey << 24) | (rpos << 18) | ((block % 8) << 8) | slots)
    bwd = _sorted((bkey << 24) | (col << 18) | ((rpos % 4) << 8) | slots)
    return fwd, bwd, offsets(fkey), offsets(bkey)


def _run_tiles(tab, bounds, tiles, tbuf, tsem, steps, prepare):
    first, end = bounds[0], bounds[-1]

    def fetch(i):
        at = lax.rem(i, NBUF)
        return pltpu.make_async_copy(tiles.at[tab[i] & 255], tbuf.at[at], tsem.at[at])

    def start(i, carry):
        fetch(i).start()
        return carry

    def run(base, width, step):
        for u in range(width):
            fetch(base + u).wait()
        for u in range(width):
            step(tab[base + u], tbuf.at[lax.rem(base + u, NBUF)])
        for u in range(width):

            @pl.when(base + u + NBUF < end)
            def _():
                fetch(base + u + NBUF).start()

    lax.fori_loop(first, jnp.minimum(first + NBUF, end), start, 0)
    prepare()
    for lo, hi, step in zip(bounds[:-1], bounds[1:], steps):
        whole = (hi - lo) // UNROLL

        def many(g, carry, lo=lo, step=step):
            run(lo + g * UNROLL, UNROLL, step)
            return carry

        lax.fori_loop(0, whole, many, 0)
        at = lo + whole * UNROLL
        width = UNROLL // 2
        while width:
            take = ((hi - at) & width) != 0

            @pl.when(take)
            def _(at=at, width=width, step=step):
                run(at, width, step)

            at = at + jnp.where(take, width, 0)
            width //= 2


def _forward_kernel(chunk, tab, offs, tiles, fa, fb, *refs):
    if chunk:
        refs = refs[1:]
    acc, tbuf, tsem = refs

    def step(feats):
        def go(word, tile):
            r = (word >> 18) & 7
            acc[r] += jnp.dot(tile[...], feats[(word >> 8) & 7], preferred_element_type=F32)

        return go

    def prepare():
        if not chunk:
            acc[...] = jnp.zeros_like(acc)

    bounds = [offs[2 * chunk + k] for k in range(3)]
    _run_tiles(tab, bounds, tiles, tbuf, tsem, [step(fa), step(fb)], prepare)


ANY = pl.BlockSpec(memory_space=pl.ANY)
HBM = pl.BlockSpec(memory_space=pltpu.HBM)
SMEM = pl.BlockSpec(memory_space=pltpu.SMEM)
VMEM = pl.BlockSpec(memory_space=pltpu.VMEM)


def _cost(extra):
    return pl.CostEstimate(
        flops=B**3, bytes_accessed=B * B, transcendentals=0
    )


def forward(chunk, tab, offs, tiles, fa, fb, acc):
    args = [tab, offs, tiles, fa, fb] + ([acc] if chunk else [])
    return pl.pallas_call(
        functools.partial(_forward_kernel, chunk),
        name=f"tiles_forward_{chunk}",
        in_specs=[SMEM, SMEM, HBM] + [VMEM] * (len(args) - 3),
        out_specs=VMEM,
        out_shape=jax.ShapeDtypeStruct((8, B, B), F32),
        input_output_aliases={5: 0} if chunk else {},
        scratch_shapes=[
            pltpu.VMEM((NBUF, B, B), BF16),
            pltpu.SemaphoreType.DMA((NBUF,)),
        ],
        compiler_params=pltpu.CompilerParams(vmem_limit_bytes=16 * MIB),
        cost_estimate=_cost(6 * MIB),
    )(*args)


def _backward_kernel(chunk, nadd, tab, offs, tiles, d0, d1, *refs):
    adds, refs = refs[:nadd], refs[nadd:]
    oa, ob, acc, tbuf, tsem = refs

    def step(dagg):
        def go(word, tile):
            f = (word >> 18) & 15
            acc[f] += jnp.dot(dagg[(word >> 8) & 3], tile[...], preferred_element_type=F32)

        return go

    def prepare():
        if chunk == 2:
            acc[0:8] = adds[0][...].astype(F32)
            acc[8:16] = adds[1][...].astype(F32)
        else:
            acc[...] = jnp.zeros_like(acc)

    bounds = [offs[2 * chunk + k] for k in range(3)]
    _run_tiles(tab, bounds, tiles, tbuf, tsem, [step(d0), step(d1)], prepare)
    if chunk != 1:
        oa[...] = acc[0:8].astype(BF16)
        ob[...] = acc[8:16].astype(BF16)
    else:
        for k in range(8):
            oa[k * B : (k + 1) * B] = acc[k].astype(BF16)
            ob[k * B : (k + 1) * B] = acc[8 + k].astype(BF16)
        oa[8 * B :] = adds[0][...]
        ob[8 * B :] = adds[0][...]


def backward(chunk, tab, offs, tiles, d0, d1, adds=()):
    shape = (8 * B + B // 2, B) if chunk == 1 else (8, B, B)
    return pl.pallas_call(
        functools.partial(_backward_kernel, chunk, len(adds)),
        name=f"tiles_backward_{chunk}",
        in_specs=[SMEM, SMEM, HBM, VMEM, VMEM] + [VMEM] * len(adds),
        out_specs=[VMEM] * 2,
        out_shape=[jax.ShapeDtypeStruct(shape, BF16)] * 2,
        scratch_shapes=[
            pltpu.VMEM((16, B, B), F32),
            pltpu.VMEM((NBUF, B, B), BF16),
            pltpu.SemaphoreType.DMA((NBUF,)),
        ],
        compiler_params=pltpu.CompilerParams(vmem_limit_bytes=24 * MIB),
        cost_estimate=_cost(6 * MIB),
    )(tab, offs, tiles, d0, d1, *adds)


def _dense_kernel(near, far, cot0, cot1, w_ref, act, dagg, wterm):
    w = w_ref[...]
    for k in range(4):
        agg = (near[k].astype(F32) + far[(k + 2) % 4].astype(F32)).astype(BF16)
        pre = jnp.dot(agg, w, preferred_element_type=F32)
        sig = jax.nn.sigmoid(pre)
        cot = (cot0 if k < 2 else cot1)[k % 2].astype(F32)
        dpre = (cot * sig * (1.0 + pre * (1.0 - sig))).astype(BF16)
        dagg[k] = lax.dot_general(
            w, dpre, (((1,), (1,)), ((), ())), preferred_element_type=F32
        ).astype(BF16)
        term = lax.dot_general(agg, dpre, (((0,), (0,)), ((), ())), preferred_element_type=F32)
        if k < 2:
            act[k] = (pre * sig).astype(BF16)
        if k % 2 == 0:
            wterm[k // 2] = term
        else:
            wterm[k // 2] = wterm[k // 2] + term


def dense(near, far, cot0, cot1, w):
    return pl.pallas_call(
        _dense_kernel,
        name="dense",
        in_specs=[VMEM] * 5,
        out_specs=[VMEM] * 3,
        out_shape=[
            jax.ShapeDtypeStruct((2, B, B), BF16),
            jax.ShapeDtypeStruct((4, B, B), BF16),
            jax.ShapeDtypeStruct((2, B, B), F32),
        ],
        compiler_params=pltpu.CompilerParams(vmem_limit_bytes=16 * MIB),
        cost_estimate=pl.CostEstimate(
            flops=10 * 2 * B**3, bytes_accessed=5 * MIB, transcendentals=1024 * 256
        ),
    )(near, far, cot0, cot1, w)


def plus(*terms):
    total = terms[0].astype(F32)
    for t in terms[1:]:
        total = total + t.astype(F32)
    return total.astype(BF16)


def blocks(rows):
    return rows.reshape(-1, B, B)


def carry(value, w):
    return jnp.concatenate([value.reshape(-1, B), w])


def ring_sum(own, across, left, right, kind=BF16):
    own, across, left, right = (t.astype(F32) for t in (own, across, left, right))
    return ((own + across) + (left + right)).astype(kind)


def body(node_feats, weight, cotangent, tiles, tile_rows, tile_cols, tile_count):
    node, rep = lax.axis_index("node"), lax.axis_index("rep")
    x, yl, z = node % NX, node // NX % NYL, node // (NX * NYL)
    c, yh = rep % NC, rep // NC
    tiles = pltpu.with_memory_space_constraint(tiles[0, 0], pltpu.HBM)
    fwd, bwd, foffs, boffs = tables(
        tile_rows[0, 0], tile_cols[0, 0], tile_count[0, 0], z, yl, x, yh, c
    )
    own = lax.dynamic_slice_in_dim(node_feats.reshape(8, B, B), rep * 2, 2, 0)
    cot0 = cotangent.reshape(2, B, B)

    pair = jnp.concatenate([own, send(own, YN)])
    lo = jnp.concatenate([pair, send(pair, UP)])
    hi = jnp.concatenate([send(pair, UM), send(pair, U2)])
    p1, m1 = send(lo, VP), send(lo, VM)
    p2, m2 = send(hi, VP), send(hi, VM)
    acc = forward(0, fwd, foffs, tiles, lo, hi, None)
    cot1 = send(tie(cot0, lo, hi), YH)
    p1, m1, acc = lax.optimization_barrier((p1, m1, acc))
    p3 = send(p1, VP)
    acc = forward(1, fwd, foffs, tiles, p1, m1, acc)
    p2, m2, acc, cot1 = lax.optimization_barrier((p2, m2, acc, cot1))
    m3 = send(m2, VM)
    acc = forward(2, fwd, foffs, tiles, p2, m2, acc)
    acc = forward(3, fwd, foffs, tiles, p3, m3, acc)

    core = send(acc[4:], CC)
    part = (acc[:4] + core).astype(BF16)
    across = send(part, YH)
    act, d0, term = dense(part, across, cot0, cot1, weight)

    half = B // 2
    whole = term[0] + term[1]
    keep = lax.dynamic_slice_in_dim(whole, c * half, half, 0)
    give = lax.dynamic_slice_in_dim(whole, (1 - c) * half, half, 0)
    d1, got = lax.optimization_barrier((send(d0, CC), send(give, CC)))
    w = keep + got

    fa, fb = backward(3, bwd, boffs, tiles, d0, d1)
    ra, rb = send(fa, VP), send(fb, VM)
    d0, d1, fa, fb, w = lax.optimization_barrier((d0, d1, fa, fb, w))
    w1 = send(w, YN)
    lo, hi = backward(0, bwd, boffs, tiles, d0, d1)
    d0, d1, lo, hi, w1 = lax.optimization_barrier((d0, d1, lo, hi, w1))
    w = (w + w1).astype(BF16)
    w2 = send(w, V2)
    m1, p1 = backward(1, bwd, boffs, tiles, d0, d1, (w,))
    s_hi, s_lo = send(p1, VP), send(m1, VM)
    d0, d1, m1, p1, ra, rb = lax.optimization_barrier((d0, d1, m1, p1, ra, rb))
    m2, p2 = backward(2, bwd, boffs, tiles, d0, d1, (rb, ra))
    t_lo, t_hi = send(p2, VP), send(m2, VM)
    s_lo, s_hi, w2 = lax.optimization_barrier((s_lo, s_hi, w2))
    w = ring_sum(w, w2, s_hi[8 * B :], s_lo[8 * B :])
    s_lo, s_hi = blocks(s_lo[: 8 * B]), blocks(s_hi[: 8 * B])
    up = carry(plus(hi[:4], s_hi[:4], t_hi[:4]), w)
    two = carry(plus(hi[4:], s_hi[4:], t_hi[4:]), w)
    down = carry(plus(lo[4:], s_lo[4:], t_lo[4:]), w)
    home = plus(lo[:4], s_lo[:4], t_lo[:4])
    from_up, from_down, from_two = send(up, UP), send(down, UM), send(two, U2)
    rest = [from_up, from_down, from_two]
    total = plus(home, *(blocks(r[: 4 * B]) for r in rest))
    other = send(total[2:], YN)
    w = ring_sum(w, *(r[4 * B :] for r in (from_two, from_up, from_down)), F32)
    got = send(w, CC)
    total = total[:2].astype(F32) + other.astype(F32)
    feature_grad = jnp.swapaxes(total, 1, 2).astype(BF16).reshape(2 * B, B)
    scale = float(node_feats.shape[0] * NZ * NYL * NX) ** (-0.5)
    weight_grad = jnp.where(
        c == 0, jnp.concatenate([w, got]), jnp.concatenate([got, w])
    ) * scale
    return act.reshape(2 * B, B), feature_grad, weight_grad


def solution(mesh):
    placed = (
        P("node", None),
        P(),
        P(("node", "rep"), None),
        P("node", "rep", None, None, None),
        P("node", "rep", None),
        P("node", "rep", None),
        P("node", "rep"),
    )
    return jax.shard_map(
        body,
        mesh=mesh,
        in_specs=placed,
        out_specs=(P(("node", "rep"), None), P(("node", "rep"), None), P()),
        check_vma=False,
    )
```

```python
import functools

import jax
import jax.numpy as jnp
from jax import lax
from jax.experimental import pallas as pl
from jax.experimental.pallas import tpu as pltpu
from jax.sharding import PartitionSpec as P

AXES = ("node", "rep")
NZ, NYL, NX, NYH, NC = 4, 2, 4, 2, 2
B = 256
F32, BF16, I32 = jnp.float32, jnp.bfloat16, jnp.int32
NBUF = 32
UNROLL = 4
MIB = 1 << 20


def _flat(z, yl, x, yh, c):
    return ((((z % NZ) * NYL + yl) * NX + x % NX) * NYH + yh) * NC + c


def _perm(move):
    pairs = []
    for z in range(NZ):
        for yl in range(NYL):
            for x in range(NX):
                for yh in range(NYH):
                    for c in range(NC):
                        pairs.append((_flat(z, yl, x, yh, c), _flat(*move(z, yl, x, yh, c))))
    return pairs


def _along(first, step):
    def move(z, yl, x, yh, c):
        if (c == 0) == first:
            return z, yl, step(x), yh, c
        return step(z), yl, x, yh, c

    return _perm(move)


UP, UM, U2 = (_along(True, lambda k, d=d: k + d) for d in (1, -1, 2))
VP, VM, V2 = (_along(False, lambda k, d=d: k + d) for d in (1, -1, 2))
YN = _perm(lambda z, yl, x, yh, c: (z, 1 - yl, x, yh, c))
YH = _perm(lambda z, yl, x, yh, c: (z, yl, x, 1 - yh, c))
CC = _perm(lambda z, yl, x, yh, c: (z, yl, x, yh, 1 - c))


def send(value, pairs):
    return lax.ppermute(value, AXES, pairs)


def tie(value, *deps):
    return lax.optimization_barrier((value, *deps))[0]


def _sorted(v):
    n = v.shape[0]
    rank = jnp.sum((v[None, :] < v[:, None]).astype(I32), axis=1)
    hit = rank[:, None] == jnp.arange(n, dtype=I32)[None, :]
    return jnp.sum(jnp.where(hit, v[:, None], 0), axis=0)


def tables(rows, cols, count, z, yl, x, yh, c):
    slots = jnp.arange(rows.shape[0], dtype=I32)
    live = slots < count
    j = cols % 2
    xr = (cols // 2 % NX - x) % NX
    yr = (cols // (2 * NX) % NYL) ^ yl
    zr = (cols // (2 * NX * NYL) - z) % NZ
    ur = jnp.where(c == 0, xr, zr)
    vr = jnp.where(c == 0, zr, xr)
    at = jnp.where(ur == 0, 0, jnp.where(ur == 3, 1, jnp.where(ur == 1, 2, 3)))
    block = at * 2 + j
    h = yr
    far = jnp.where(vr == 2, 6 + h, jnp.where(vr == 3, 2 + 2 * h, h))
    seg = jnp.where(vr == 1, 3 + 2 * h, far)
    bseg = jnp.where(vr == 1, 5 - 2 * h, far)
    q = rows // 2
    rpos = ((q % 2) ^ c) * 4 + ((q // 2) ^ yh) * 2 + rows % 2
    ends = jnp.arange(9, dtype=I32)[:, None]

    def offsets(key):
        return jnp.sum((key[None, :] < ends).astype(I32), axis=1)

    fkey = jnp.where(live, seg, 8)
    bkey = jnp.where(live, (bseg // 2) * 2 + rpos // 4, 8)
    col = (bseg % 2) * 8 + block
    fwd = _sorted((fkey << 24) | (rpos << 18) | (block << 8) | slots)
    bwd = _sorted((bkey << 24) | (col << 18) | ((rpos % 4) << 8) | slots)
    return fwd, bwd, offsets(fkey), offsets(bkey)


def _run_tiles(tab, bounds, tiles, tbuf, tsem, steps, prepare):
    first, end = bounds[0], bounds[-1]

    def fetch(i):
        at = lax.rem(i, NBUF)
        return pltpu.make_async_copy(tiles.at[tab[i] & 255], tbuf.at[at], tsem.at[at])

    def start(i, carry):
        fetch(i).start()
        return carry

    def run(base, width, step):
        for u in range(width):
            fetch(base + u).wait()
        for u in range(width):
            step(tab[base + u], tbuf.at[lax.rem(base + u, NBUF)])
        for u in range(width):

            @pl.when(base + u + NBUF < end)
            def _():
                fetch(base + u + NBUF).start()

    lax.fori_loop(first, jnp.minimum(first + NBUF, end), start, 0)
    prepare()
    for lo, hi, step in zip(bounds[:-1], bounds[1:], steps):
        whole = (hi - lo) // UNROLL

        def many(g, carry, lo=lo, step=step):
            run(lo + g * UNROLL, UNROLL, step)
            return carry

        lax.fori_loop(0, whole, many, 0)
        at = lo + whole * UNROLL
        width = UNROLL // 2
        while width:
            take = ((hi - at) & width) != 0

            @pl.when(take)
            def _(at=at, width=width, step=step):
                run(at, width, step)

            at = at + jnp.where(take, width, 0)
            width //= 2


def _forward_kernel(chunk, tab, offs, tiles, fa, fb, *refs):
    if chunk:
        refs = refs[1:]
    acc, tbuf, tsem = refs

    def step(feats):
        def go(word, tile):
            r = (word >> 18) & 7
            acc[r] += jnp.dot(tile[...], feats[(word >> 8) & 7], preferred_element_type=F32)

        return go

    def prepare():
        if not chunk:
            acc[...] = jnp.zeros_like(acc)

    bounds = [offs[2 * chunk + k] for k in range(3)]
    _run_tiles(tab, bounds, tiles, tbuf, tsem, [step(fa), step(fb)], prepare)


ANY = pl.BlockSpec(memory_space=pl.ANY)
HBM = pl.BlockSpec(memory_space=pltpu.HBM)
SMEM = pl.BlockSpec(memory_space=pltpu.SMEM)
VMEM = pl.BlockSpec(memory_space=pltpu.VMEM)


def _cost(extra):
    return pl.CostEstimate(
        flops=B**3, bytes_accessed=B * B, transcendentals=0
    )


def forward(chunk, tab, offs, tiles, fa, fb, acc):
    args = [tab, offs, tiles, fa, fb] + ([acc] if chunk else [])
    return pl.pallas_call(
        functools.partial(_forward_kernel, chunk),
        name=f"tiles_forward_{chunk}",
        in_specs=[SMEM, SMEM, HBM] + [VMEM] * (len(args) - 3),
        out_specs=VMEM,
        out_shape=jax.ShapeDtypeStruct((8, B, B), F32),
        input_output_aliases={5: 0} if chunk else {},
        scratch_shapes=[
            pltpu.VMEM((NBUF, B, B), BF16),
            pltpu.SemaphoreType.DMA((NBUF,)),
        ],
        compiler_params=pltpu.CompilerParams(vmem_limit_bytes=16 * MIB),
        cost_estimate=_cost(6 * MIB),
    )(*args)


def _backward_kernel(chunk, nadd, tab, offs, tiles, d0, d1, *refs):
    adds, refs = refs[:nadd], refs[nadd:]
    oa, ob, acc, tbuf, tsem = refs

    def step(dagg):
        def go(word, tile):
            f = (word >> 18) & 15
            acc[f] += jnp.dot(dagg[(word >> 8) & 3], tile[...], preferred_element_type=F32)

        return go

    def prepare():
        if chunk == 2:
            acc[0:8] = adds[0][...].astype(F32)
            acc[8:16] = adds[1][...].astype(F32)
        else:
            acc[...] = jnp.zeros_like(acc)

    bounds = [offs[2 * chunk + k] for k in range(3)]
    _run_tiles(tab, bounds, tiles, tbuf, tsem, [step(d0), step(d1)], prepare)
    if chunk != 1:
        oa[...] = acc[0:8].astype(BF16)
        ob[...] = acc[8:16].astype(BF16)
    else:
        for k in range(8):
            oa[k * B : (k + 1) * B] = acc[k].astype(BF16)
            ob[k * B : (k + 1) * B] = acc[8 + k].astype(BF16)
        oa[8 * B :] = adds[0][...]
        ob[8 * B :] = adds[0][...]


def backward(chunk, tab, offs, tiles, d0, d1, adds=()):
    shape = (8 * B + B // 2, B) if chunk == 1 else (8, B, B)
    return pl.pallas_call(
        functools.partial(_backward_kernel, chunk, len(adds)),
        name=f"tiles_backward_{chunk}",
        in_specs=[SMEM, SMEM, HBM, VMEM, VMEM] + [VMEM] * len(adds),
        out_specs=[VMEM] * 2,
        out_shape=[jax.ShapeDtypeStruct(shape, BF16)] * 2,
        scratch_shapes=[
            pltpu.VMEM((16, B, B), F32),
            pltpu.VMEM((NBUF, B, B), BF16),
            pltpu.SemaphoreType.DMA((NBUF,)),
        ],
        compiler_params=pltpu.CompilerParams(vmem_limit_bytes=24 * MIB),
        cost_estimate=_cost(6 * MIB),
    )(tab, offs, tiles, d0, d1, *adds)


def _dense_kernel(near, far, cot0, cot1, w_ref, act, dagg, wterm):
    w = w_ref[...]
    for k in range(4):
        agg = (near[k].astype(F32) + far[(k + 2) % 4].astype(F32)).astype(BF16)
        pre = jnp.dot(agg, w, preferred_element_type=F32)
        sig = jax.nn.sigmoid(pre)
        cot = (cot0 if k < 2 else cot1)[k % 2].astype(F32)
        dpre = (cot * sig * (1.0 + pre * (1.0 - sig))).astype(BF16)
        dagg[k] = lax.dot_general(
            w, dpre, (((1,), (1,)), ((), ())), preferred_element_type=F32
        ).astype(BF16)
        term = lax.dot_general(agg, dpre, (((0,), (0,)), ((), ())), preferred_element_type=F32)
        if k < 2:
            act[k] = (pre * sig).astype(BF16)
        if k % 2 == 0:
            wterm[k // 2] = term
        else:
            wterm[k // 2] = wterm[k // 2] + term


def dense(near, far, cot0, cot1, w):
    return pl.pallas_call(
        _dense_kernel,
        name="dense",
        in_specs=[VMEM] * 5,
        out_specs=[VMEM] * 3,
        out_shape=[
            jax.ShapeDtypeStruct((2, B, B), BF16),
            jax.ShapeDtypeStruct((4, B, B), BF16),
            jax.ShapeDtypeStruct((2, B, B), F32),
        ],
        compiler_params=pltpu.CompilerParams(vmem_limit_bytes=16 * MIB),
        cost_estimate=pl.CostEstimate(
            flops=10 * 2 * B**3, bytes_accessed=5 * MIB, transcendentals=1024 * 256
        ),
    )(near, far, cot0, cot1, w)


def plus(*terms):
    total = terms[0].astype(F32)
    for t in terms[1:]:
        total = total + t.astype(F32)
    return total.astype(BF16)


def blocks(rows):
    return rows.reshape(-1, B, B)


def carry(value, w):
    return jnp.concatenate([value.reshape(-1, B), w])


def ring_sum(own, across, left, right, kind=BF16):
    own, across, left, right = (t.astype(F32) for t in (own, across, left, right))
    return ((own + across) + (left + right)).astype(kind)


def body(node_feats, weight, cotangent, tiles, tile_rows, tile_cols, tile_count):
    node, rep = lax.axis_index("node"), lax.axis_index("rep")
    x, yl, z = node % NX, node // NX % NYL, node // (NX * NYL)
    c, yh = rep % NC, rep // NC
    tiles = pltpu.with_memory_space_constraint(tiles[0, 0], pltpu.HBM)
    fwd, bwd, foffs, boffs = tables(
        tile_rows[0, 0], tile_cols[0, 0], tile_count[0, 0], z, yl, x, yh, c
    )
    own = lax.dynamic_slice_in_dim(node_feats.reshape(8, B, B), rep * 2, 2, 0)
    cot0 = cotangent.reshape(2, B, B)

    def ring(t):
        return jnp.concatenate([t, send(t, UP), send(t, UM), send(t, U2)])

    other = send(own, YN)
    lo, hi = ring(own), ring(other)
    cot1 = send(tie(cot0, other), YH)
    hi, cot1 = lax.optimization_barrier((hi, cot1))
    p1, m1 = send(lo, VP), send(lo, VM)
    p2, m2 = send(hi, VP), send(hi, VM)
    acc = forward(0, fwd, foffs, tiles, lo, hi, None)
    p1, m1, acc = lax.optimization_barrier((p1, m1, acc))
    p3 = send(p1, VP)
    acc = forward(1, fwd, foffs, tiles, p1, m1, acc)
    p2, m2, acc = lax.optimization_barrier((p2, m2, acc))
    m3 = send(m2, VM)
    acc = forward(2, fwd, foffs, tiles, p2, m2, acc)
    acc = forward(3, fwd, foffs, tiles, p3, m3, acc)

    core = send(acc[4:], CC)
    part = (acc[:4] + core).astype(BF16)
    across = send(part, YH)
    act, d0, term = dense(part, across, cot0, cot1, weight)

    half = B // 2
    whole = term[0] + term[1]
    keep = lax.dynamic_slice_in_dim(whole, c * half, half, 0)
    give = lax.dynamic_slice_in_dim(whole, (1 - c) * half, half, 0)
    d1, got = lax.optimization_barrier((send(d0, CC), send(give, CC)))
    w = keep + got

    fa, fb = backward(3, bwd, boffs, tiles, d0, d1)
    ra, rb = send(fa, VP), send(fb, VM)
    d0, d1, fa, fb, w = lax.optimization_barrier((d0, d1, fa, fb, w))
    w1 = send(w, YN)
    lo, hi = backward(0, bwd, boffs, tiles, d0, d1)
    d0, d1, lo, hi, w1 = lax.optimization_barrier((d0, d1, lo, hi, w1))
    w = (w + w1).astype(BF16)
    w2 = send(w, V2)
    m1, p1 = backward(1, bwd, boffs, tiles, d0, d1, (w,))
    s_hi, s_lo = send(p1, VP), send(m1, VM)
    d0, d1, m1, p1, ra, rb = lax.optimization_barrier((d0, d1, m1, p1, ra, rb))
    m2, p2 = backward(2, bwd, boffs, tiles, d0, d1, (rb, ra))
    t_lo, t_hi = send(p2, VP), send(m2, VM)
    s_lo, s_hi, w2 = lax.optimization_barrier((s_lo, s_hi, w2))
    w = ring_sum(w, w2, s_hi[8 * B :], s_lo[8 * B :])
    s_lo, s_hi = blocks(s_lo[: 8 * B]), blocks(s_hi[: 8 * B])
    def spread(own, s, t, extra):
        near, down, up, two = (plus(own[k : k + 2], s[k : k + 2], t[k : k + 2]) for k in (0, 2, 4, 6))
        if extra is not None:
            down, up, two = (carry(v, extra) for v in (down, up, two))
        return near, send(two, U2), send(up, UP), send(down, UM)

    far, *rest = spread(hi, s_hi, t_hi, w)
    near, *parts = spread(lo, s_lo, t_lo, None)
    far = plus(far, *(blocks(r[: 2 * B]) for r in rest))
    w = ring_sum(w, *(r[2 * B :] for r in rest), F32)
    other = send(far, YN)
    got = send(w, CC)
    total = sum((t.astype(F32) for t in (near, *parts, other)), jnp.zeros((), F32))
    feature_grad = jnp.swapaxes(total, 1, 2).astype(BF16).reshape(2 * B, B)
    scale = float(node_feats.shape[0] * NZ * NYL * NX) ** (-0.5)
    weight_grad = jnp.where(
        c == 0, jnp.concatenate([w, got]), jnp.concatenate([got, w])
    ) * scale
    return act.reshape(2 * B, B), feature_grad, weight_grad


def solution(mesh):
    placed = (
        P("node", None),
        P(),
        P(("node", "rep"), None),
        P("node", "rep", None, None, None),
        P("node", "rep", None),
        P("node", "rep", None),
        P("node", "rep"),
    )
    return jax.shard_map(
        body,
        mesh=mesh,
        in_specs=placed,
        out_specs=(P(("node", "rep"), None), P(("node", "rep"), None), P()),
        check_vma=False,
    )
```

```python
import functools

import jax
import jax.numpy as jnp
from jax import lax
from jax.experimental import pallas as pl
from jax.experimental.pallas import tpu as pltpu
from jax.sharding import PartitionSpec as P

AXES = ("node", "rep")
NZ, NYL, NX, NYH, NC = 4, 2, 4, 2, 2
B = 256
F32, BF16, I32 = jnp.float32, jnp.bfloat16, jnp.int32
NBUF = 32
UNROLL = 4
MIB = 1 << 20


def _flat(z, yl, x, yh, c):
    return ((((z % NZ) * NYL + yl) * NX + x % NX) * NYH + yh) * NC + c


def _perm(move):
    pairs = []
    for z in range(NZ):
        for yl in range(NYL):
            for x in range(NX):
                for yh in range(NYH):
                    for c in range(NC):
                        pairs.append((_flat(z, yl, x, yh, c), _flat(*move(z, yl, x, yh, c))))
    return pairs


def _along(first, step):
    def move(z, yl, x, yh, c):
        if (c == 0) == first:
            return z, yl, step(x), yh, c
        return step(z), yl, x, yh, c

    return _perm(move)


UP, UM, U2 = (_along(True, lambda k, d=d: k + d) for d in (1, -1, 2))
VP, VM, V2 = (_along(False, lambda k, d=d: k + d) for d in (1, -1, 2))
YN = _perm(lambda z, yl, x, yh, c: (z, 1 - yl, x, yh, c))
YH = _perm(lambda z, yl, x, yh, c: (z, yl, x, 1 - yh, c))
CC = _perm(lambda z, yl, x, yh, c: (z, yl, x, yh, 1 - c))


def send(value, pairs):
    return lax.ppermute(value, AXES, pairs)


def tie(value, *deps):
    return lax.optimization_barrier((value, *deps))[0]


def _sorted(v):
    n = v.shape[0]
    rank = jnp.sum((v[None, :] < v[:, None]).astype(I32), axis=1)
    hit = rank[:, None] == jnp.arange(n, dtype=I32)[None, :]
    return jnp.sum(jnp.where(hit, v[:, None], 0), axis=0)


def tables(rows, cols, count, z, yl, x, yh, c):
    slots = jnp.arange(rows.shape[0], dtype=I32)
    live = slots < count
    j = cols % 2
    xr = (cols // 2 % NX - x) % NX
    yr = (cols // (2 * NX) % NYL) ^ yl
    zr = (cols // (2 * NX * NYL) - z) % NZ
    ur = jnp.where(c == 0, xr, zr)
    vr = jnp.where(c == 0, zr, xr)
    at = jnp.where(ur == 0, 0, jnp.where(ur == 3, 1, jnp.where(ur == 1, 2, 3)))
    block = at * 2 + j
    h = yr
    far = jnp.where(vr == 2, 6 + h, jnp.where(vr == 3, 2 + 2 * h, h))
    seg = jnp.where(vr == 1, 3 + 2 * h, far)
    bseg = jnp.where(vr == 1, 5 - 2 * h, far)
    q = rows // 2
    rpos = ((q % 2) ^ c) * 4 + ((q // 2) ^ yh) * 2 + rows % 2
    ends = jnp.arange(9, dtype=I32)[:, None]

    def offsets(key):
        return jnp.sum((key[None, :] < ends).astype(I32), axis=1)

    fkey = jnp.where(live, seg, 8)
    bkey = jnp.where(live, (bseg // 2) * 2 + rpos // 4, 8)
    col = (bseg % 2) * 8 + block
    fwd = _sorted((fkey << 24) | (rpos << 18) | (block << 8) | slots)
    bwd = _sorted((bkey << 24) | (col << 18) | ((rpos % 4) << 8) | slots)
    return fwd, bwd, offsets(fkey), offsets(bkey)


def _run_tiles(tab, bounds, tiles, tbuf, tsem, steps, prepare):
    first, end = bounds[0], bounds[-1]

    def fetch(i):
        at = lax.rem(i, NBUF)
        return pltpu.make_async_copy(tiles.at[tab[i] & 255], tbuf.at[at], tsem.at[at])

    def start(i, carry):
        fetch(i).start()
        return carry

    def run(base, width, step):
        for u in range(width):
            fetch(base + u).wait()
        for u in range(width):
            step(tab[base + u], tbuf.at[lax.rem(base + u, NBUF)])
        for u in range(width):

            @pl.when(base + u + NBUF < end)
            def _():
                fetch(base + u + NBUF).start()

    lax.fori_loop(first, jnp.minimum(first + NBUF, end), start, 0)
    prepare()
    for lo, hi, step in zip(bounds[:-1], bounds[1:], steps):
        whole = (hi - lo) // UNROLL

        def many(g, carry, lo=lo, step=step):
            run(lo + g * UNROLL, UNROLL, step)
            return carry

        lax.fori_loop(0, whole, many, 0)
        at = lo + whole * UNROLL
        width = UNROLL // 2
        while width:
            take = ((hi - at) & width) != 0

            @pl.when(take)
            def _(at=at, width=width, step=step):
                run(at, width, step)

            at = at + jnp.where(take, width, 0)
            width //= 2


def _forward_kernel(chunk, tab, offs, tiles, fa, fb, *refs):
    if chunk:
        refs = refs[1:]
    acc, tbuf, tsem = refs

    def step(feats):
        def go(word, tile):
            r = (word >> 18) & 7
            acc[r] += jnp.dot(tile[...], feats[(word >> 8) & 7], preferred_element_type=F32)

        return go

    def prepare():
        if not chunk:
            acc[...] = jnp.zeros_like(acc)

    bounds = [offs[2 * chunk + k] for k in range(3)]
    _run_tiles(tab, bounds, tiles, tbuf, tsem, [step(fa), step(fb)], prepare)


ANY = pl.BlockSpec(memory_space=pl.ANY)
HBM = pl.BlockSpec(memory_space=pltpu.HBM)
SMEM = pl.BlockSpec(memory_space=pltpu.SMEM)
VMEM = pl.BlockSpec(memory_space=pltpu.VMEM)


def _cost(extra):
    return pl.CostEstimate(
        flops=B**3, bytes_accessed=B * B, transcendentals=0
    )


def forward(chunk, tab, offs, tiles, fa, fb, acc):
    args = [tab, offs, tiles, fa, fb] + ([acc] if chunk else [])
    return pl.pallas_call(
        functools.partial(_forward_kernel, chunk),
        name=f"tiles_forward_{chunk}",
        in_specs=[SMEM, SMEM, HBM] + [VMEM] * (len(args) - 3),
        out_specs=VMEM,
        out_shape=jax.ShapeDtypeStruct((8, B, B), F32),
        input_output_aliases={5: 0} if chunk else {},
        scratch_shapes=[
            pltpu.VMEM((NBUF, B, B), BF16),
            pltpu.SemaphoreType.DMA((NBUF,)),
        ],
        compiler_params=pltpu.CompilerParams(vmem_limit_bytes=16 * MIB),
        cost_estimate=_cost(6 * MIB),
    )(*args)


def _backward_kernel(chunk, nadd, tab, offs, tiles, d0, d1, *refs):
    adds, refs = refs[:nadd], refs[nadd:]
    oa, ob, acc, tbuf, tsem = refs

    def step(dagg):
        def go(word, tile):
            f = (word >> 18) & 15
            acc[f] += jnp.dot(dagg[(word >> 8) & 3], tile[...], preferred_element_type=F32)

        return go

    def prepare():
        if chunk == 2:
            acc[0:8] = adds[0][...].astype(F32)
            acc[8:16] = adds[1][...].astype(F32)
        else:
            acc[...] = jnp.zeros_like(acc)

    bounds = [offs[2 * chunk + k] for k in range(3)]
    _run_tiles(tab, bounds, tiles, tbuf, tsem, [step(d0), step(d1)], prepare)
    if chunk != 1:
        oa[...] = acc[0:8].astype(BF16)
        ob[...] = acc[8:16].astype(BF16)
    else:
        for k in range(8):
            oa[k * B : (k + 1) * B] = acc[k].astype(BF16)
            ob[k * B : (k + 1) * B] = acc[8 + k].astype(BF16)
        oa[8 * B :] = adds[0][...]
        ob[8 * B :] = adds[0][...]


def backward(chunk, tab, offs, tiles, d0, d1, adds=()):
    shape = (8 * B + B // 2, B) if chunk == 1 else (8, B, B)
    return pl.pallas_call(
        functools.partial(_backward_kernel, chunk, len(adds)),
        name=f"tiles_backward_{chunk}",
        in_specs=[SMEM, SMEM, HBM, VMEM, VMEM] + [VMEM] * len(adds),
        out_specs=[VMEM] * 2,
        out_shape=[jax.ShapeDtypeStruct(shape, BF16)] * 2,
        scratch_shapes=[
            pltpu.VMEM((16, B, B), F32),
            pltpu.VMEM((NBUF, B, B), BF16),
            pltpu.SemaphoreType.DMA((NBUF,)),
        ],
        compiler_params=pltpu.CompilerParams(vmem_limit_bytes=24 * MIB),
        cost_estimate=_cost(6 * MIB),
    )(tab, offs, tiles, d0, d1, *adds)


def _dense_kernel(near, far, cot0, cot1, w_ref, act, dagg, wterm):
    w = w_ref[...]
    for k in range(4):
        agg = (near[k].astype(F32) + far[(k + 2) % 4].astype(F32)).astype(BF16)
        pre = jnp.dot(agg, w, preferred_element_type=F32)
        sig = jax.nn.sigmoid(pre)
        cot = (cot0 if k < 2 else cot1)[k % 2].astype(F32)
        dpre = (cot * sig * (1.0 + pre * (1.0 - sig))).astype(BF16)
        dagg[k] = lax.dot_general(
            w, dpre, (((1,), (1,)), ((), ())), preferred_element_type=F32
        ).astype(BF16)
        term = lax.dot_general(agg, dpre, (((0,), (0,)), ((), ())), preferred_element_type=F32)
        if k < 2:
            act[k] = (pre * sig).astype(BF16)
        if k % 2 == 0:
            wterm[k // 2] = term
        else:
            wterm[k // 2] = wterm[k // 2] + term


def dense(near, far, cot0, cot1, w):
    return pl.pallas_call(
        _dense_kernel,
        name="dense",
        in_specs=[VMEM] * 5,
        out_specs=[VMEM] * 3,
        out_shape=[
            jax.ShapeDtypeStruct((2, B, B), BF16),
            jax.ShapeDtypeStruct((4, B, B), BF16),
            jax.ShapeDtypeStruct((2, B, B), F32),
        ],
        compiler_params=pltpu.CompilerParams(vmem_limit_bytes=16 * MIB),
        cost_estimate=pl.CostEstimate(
            flops=10 * 2 * B**3, bytes_accessed=5 * MIB, transcendentals=1024 * 256
        ),
    )(near, far, cot0, cot1, w)


def plus(*terms):
    total = terms[0].astype(F32)
    for t in terms[1:]:
        total = total + t.astype(F32)
    return total.astype(BF16)


def blocks(rows):
    return rows.reshape(-1, B, B)


def carry(value, w):
    return jnp.concatenate([value.reshape(-1, B), w])


def ring_sum(own, across, left, right, kind=BF16):
    own, across, left, right = (t.astype(F32) for t in (own, across, left, right))
    return ((own + across) + (left + right)).astype(kind)


def body(node_feats, weight, cotangent, tiles, tile_rows, tile_cols, tile_count):
    node, rep = lax.axis_index("node"), lax.axis_index("rep")
    x, yl, z = node % NX, node // NX % NYL, node // (NX * NYL)
    c, yh = rep % NC, rep // NC
    tiles = pltpu.with_memory_space_constraint(tiles[0, 0], pltpu.HBM)
    fwd, bwd, foffs, boffs = tables(
        tile_rows[0, 0], tile_cols[0, 0], tile_count[0, 0], z, yl, x, yh, c
    )
    own = lax.dynamic_slice_in_dim(node_feats.reshape(8, B, B), rep * 2, 2, 0)
    cot0 = cotangent.reshape(2, B, B)

    def ring(t):
        return jnp.concatenate([t, send(t, UP), send(t, UM), send(t, U2)])

    other = send(own, YN)
    lo, hi = ring(own), ring(other)
    cot1 = send(tie(cot0, other), YH)
    hi, cot1 = lax.optimization_barrier((hi, cot1))
    p1, m1 = send(lo, VP), send(lo, VM)
    p2, m2 = send(hi, VP), send(hi, VM)
    acc = forward(0, fwd, foffs, tiles, lo, hi, None)
    p1, m1, acc = lax.optimization_barrier((p1, m1, acc))
    p3 = send(p1, VP)
    acc = forward(1, fwd, foffs, tiles, p1, m1, acc)
    p2, m2, acc = lax.optimization_barrier((p2, m2, acc))
    m3 = send(m2, VM)
    acc = forward(2, fwd, foffs, tiles, p2, m2, acc)
    acc = forward(3, fwd, foffs, tiles, p3, m3, acc)

    core = send(acc[4:], CC)
    part = (acc[:4] + core).astype(BF16)
    across = send(part, YH)
    act, d0, term = dense(part, across, cot0, cot1, weight)

    half = B // 2
    whole = term[0] + term[1]
    keep = lax.dynamic_slice_in_dim(whole, c * half, half, 0)
    give = lax.dynamic_slice_in_dim(whole, (1 - c) * half, half, 0)
    d1, got = lax.optimization_barrier((send(d0, CC), send(give, CC)))
    w = (keep + got).astype(BF16)

    fa, fb = backward(3, bwd, boffs, tiles, d0, d1)
    ra, rb = send(fa, VP), send(fb, VM)
    d0, d1, fa, fb, w = lax.optimization_barrier((d0, d1, fa, fb, w))
    w2 = send(w, V2)
    m1, p1 = backward(1, bwd, boffs, tiles, d0, d1, (w,))
    s_hi, s_lo = send(p1, VP), send(m1, VM)
    d0, d1, m1, p1, ra, rb = lax.optimization_barrier((d0, d1, m1, p1, ra, rb))
    m2, p2 = backward(2, bwd, boffs, tiles, d0, d1, (rb, ra))
    t_lo, t_hi = send(p2, VP), send(m2, VM)
    d0, d1, m2, p2 = lax.optimization_barrier((d0, d1, m2, p2))
    lo, hi = backward(0, bwd, boffs, tiles, d0, d1)
    s_lo, s_hi, w2 = lax.optimization_barrier((s_lo, s_hi, w2))
    w = ring_sum(w, w2, s_hi[8 * B :], s_lo[8 * B :])
    s_lo, s_hi = blocks(s_lo[: 8 * B]), blocks(s_hi[: 8 * B])
    def spread(own, s, t, extra):
        near, down, up, two = (plus(own[k : k + 2], s[k : k + 2], t[k : k + 2]) for k in (0, 2, 4, 6))
        if extra is not None:
            down, up, two = (carry(v, extra) for v in (down, up, two))
        return near, send(two, U2), send(up, UP), send(down, UM)

    far, *rest = spread(hi, s_hi, t_hi, w)
    near, *parts = spread(lo, s_lo, t_lo, None)
    far = plus(far, *(blocks(r[: 2 * B]) for r in rest))
    w = ring_sum(w, *(r[2 * B :] for r in rest))
    other = send(carry(far, w), YN)
    w = w.astype(F32) + other[2 * B :].astype(F32)
    other = blocks(other[: 2 * B])
    got = send(w, CC)
    total = sum((t.astype(F32) for t in (near, *parts, other)), jnp.zeros((), F32))
    feature_grad = jnp.swapaxes(total, 1, 2).astype(BF16).reshape(2 * B, B)
    scale = float(node_feats.shape[0] * NZ * NYL * NX) ** (-0.5)
    weight_grad = jnp.where(
        c == 0, jnp.concatenate([w, got]), jnp.concatenate([got, w])
    ) * scale
    return act.reshape(2 * B, B), feature_grad, weight_grad


def solution(mesh):
    placed = (
        P("node", None),
        P(),
        P(("node", "rep"), None),
        P("node", "rep", None, None, None),
        P("node", "rep", None),
        P("node", "rep", None),
        P("node", "rep"),
    )
    return jax.shard_map(
        body,
        mesh=mesh,
        in_specs=placed,
        out_specs=(P(("node", "rep"), None), P(("node", "rep"), None), P()),
        check_vma=False,
    )
```

```python
import functools

import jax
import jax.numpy as jnp
from jax import lax
from jax.experimental import pallas as pl
from jax.experimental.pallas import tpu as pltpu
from jax.sharding import PartitionSpec as P

AXES = ("node", "rep")
NZ, NYL, NX, NYH, NC = 4, 2, 4, 2, 2
B = 256
F32, BF16, I32 = jnp.float32, jnp.bfloat16, jnp.int32
NBUF = 32
UNROLL = 4
MIB = 1 << 20


def _flat(z, yl, x, yh, c):
    return ((((z % NZ) * NYL + yl) * NX + x % NX) * NYH + yh) * NC + c


def _perm(move):
    pairs = []
    for z in range(NZ):
        for yl in range(NYL):
            for x in range(NX):
                for yh in range(NYH):
                    for c in range(NC):
                        pairs.append((_flat(z, yl, x, yh, c), _flat(*move(z, yl, x, yh, c))))
    return pairs


def _along(first, step):
    def move(z, yl, x, yh, c):
        if (c == 0) == first:
            return z, yl, step(x), yh, c
        return step(z), yl, x, yh, c

    return _perm(move)


UP, UM, U2 = (_along(True, lambda k, d=d: k + d) for d in (1, -1, 2))
VP, VM, V2 = (_along(False, lambda k, d=d: k + d) for d in (1, -1, 2))
YN = _perm(lambda z, yl, x, yh, c: (z, 1 - yl, x, yh, c))
YH = _perm(lambda z, yl, x, yh, c: (z, yl, x, 1 - yh, c))
CC = _perm(lambda z, yl, x, yh, c: (z, yl, x, yh, 1 - c))


def send(value, pairs):
    return lax.ppermute(value, AXES, pairs)


def tie(value, *deps):
    return lax.optimization_barrier((value, *deps))[0]


def _sorted(v):
    n = v.shape[0]
    rank = jnp.sum((v[None, :] < v[:, None]).astype(I32), axis=1)
    hit = rank[:, None] == jnp.arange(n, dtype=I32)[None, :]
    return jnp.sum(jnp.where(hit, v[:, None], 0), axis=0)


def tables(rows, cols, count, z, yl, x, yh, c):
    slots = jnp.arange(rows.shape[0], dtype=I32)
    live = slots < count
    j = cols % 2
    xr = (cols // 2 % NX - x) % NX
    yr = (cols // (2 * NX) % NYL) ^ yl
    zr = (cols // (2 * NX * NYL) - z) % NZ
    ur = jnp.where(c == 0, xr, zr)
    vr = jnp.where(c == 0, zr, xr)
    at = jnp.where(ur == 0, 0, jnp.where(ur == 3, 1, jnp.where(ur == 1, 2, 3)))
    block = at * 2 + j
    h = yr
    far = jnp.where(vr == 2, 6 + h, jnp.where(vr == 3, 2 + 2 * h, h))
    seg = jnp.where(vr == 1, 3 + 2 * h, far)
    bseg = jnp.where(vr == 1, 5 - 2 * h, far)
    q = rows // 2
    rpos = ((q % 2) ^ c) * 4 + ((q // 2) ^ yh) * 2 + rows % 2
    ends = jnp.arange(9, dtype=I32)[:, None]

    def offsets(key):
        return jnp.sum((key[None, :] < ends).astype(I32), axis=1)

    fkey = jnp.where(live, seg, 8)
    bkey = jnp.where(live, (bseg // 2) * 2 + rpos // 4, 8)
    col = (bseg % 2) * 8 + block
    fwd = _sorted((fkey << 24) | (rpos << 18) | (block << 8) | slots)
    bwd = _sorted((bkey << 24) | (col << 18) | ((rpos % 4) << 8) | slots)
    return fwd, bwd, offsets(fkey), offsets(bkey)


def _run_tiles(tab, bounds, tiles, tbuf, tsem, steps, prepare):
    first, end = bounds[0], bounds[-1]

    def fetch(i):
        at = lax.rem(i, NBUF)
        return pltpu.make_async_copy(tiles.at[tab[i] & 255], tbuf.at[at], tsem.at[at])

    def start(i, carry):
        fetch(i).start()
        return carry

    def run(base, width, step):
        for u in range(width):
            fetch(base + u).wait()
        for u in range(width):
            step(tab[base + u], tbuf.at[lax.rem(base + u, NBUF)])
        for u in range(width):

            @pl.when(base + u + NBUF < end)
            def _():
                fetch(base + u + NBUF).start()

    lax.fori_loop(first, jnp.minimum(first + NBUF, end), start, 0)
    prepare()
    for lo, hi, step in zip(bounds[:-1], bounds[1:], steps):
        whole = (hi - lo) // UNROLL

        def many(g, carry, lo=lo, step=step):
            run(lo + g * UNROLL, UNROLL, step)
            return carry

        lax.fori_loop(0, whole, many, 0)
        at = lo + whole * UNROLL
        width = UNROLL // 2
        while width:
            take = ((hi - at) & width) != 0

            @pl.when(take)
            def _(at=at, width=width, step=step):
                run(at, width, step)

            at = at + jnp.where(take, width, 0)
            width //= 2


def _forward_kernel(chunk, tab, offs, tiles, fa, fb, *refs):
    if chunk:
        refs = refs[1:]
    acc, tbuf, tsem = refs

    def step(feats):
        def go(word, tile):
            r = (word >> 18) & 7
            acc[r] += jnp.dot(tile[...], feats[(word >> 8) & 7], preferred_element_type=F32)

        return go

    def prepare():
        if not chunk:
            acc[...] = jnp.zeros_like(acc)

    bounds = [offs[2 * chunk + k] for k in range(3)]
    _run_tiles(tab, bounds, tiles, tbuf, tsem, [step(fa), step(fb)], prepare)


ANY = pl.BlockSpec(memory_space=pl.ANY)
HBM = pl.BlockSpec(memory_space=pltpu.HBM)
SMEM = pl.BlockSpec(memory_space=pltpu.SMEM)
VMEM = pl.BlockSpec(memory_space=pltpu.VMEM)


def _cost(extra):
    return pl.CostEstimate(
        flops=B**3, bytes_accessed=B * B, transcendentals=0
    )


def forward(chunk, tab, offs, tiles, fa, fb, acc):
    args = [tab, offs, tiles, fa, fb] + ([acc] if chunk else [])
    return pl.pallas_call(
        functools.partial(_forward_kernel, chunk),
        name=f"tiles_forward_{chunk}",
        in_specs=[SMEM, SMEM, HBM] + [VMEM] * (len(args) - 3),
        out_specs=VMEM,
        out_shape=jax.ShapeDtypeStruct((8, B, B), F32),
        input_output_aliases={5: 0} if chunk else {},
        scratch_shapes=[
            pltpu.VMEM((NBUF, B, B), BF16),
            pltpu.SemaphoreType.DMA((NBUF,)),
        ],
        compiler_params=pltpu.CompilerParams(vmem_limit_bytes=16 * MIB),
        cost_estimate=_cost(6 * MIB),
    )(*args)


def _backward_kernel(chunk, nadd, tab, offs, tiles, d0, d1, *refs):
    adds, refs = refs[:nadd], refs[nadd:]
    oa, ob, acc, tbuf, tsem = refs

    def step(dagg):
        def go(word, tile):
            f = (word >> 18) & 15
            acc[f] += jnp.dot(dagg[(word >> 8) & 3], tile[...], preferred_element_type=F32)

        return go

    def prepare():
        if chunk == 2:
            acc[0:8] = adds[0][...].astype(F32)
            acc[8:16] = adds[1][...].astype(F32)
        else:
            acc[...] = jnp.zeros_like(acc)

    bounds = [offs[2 * chunk + k] for k in range(3)]
    _run_tiles(tab, bounds, tiles, tbuf, tsem, [step(d0), step(d1)], prepare)
    if chunk != 1:
        oa[...] = acc[0:8].astype(BF16)
        ob[...] = acc[8:16].astype(BF16)
    else:
        for k in range(8):
            oa[k * B : (k + 1) * B] = acc[k].astype(BF16)
            ob[k * B : (k + 1) * B] = acc[8 + k].astype(BF16)
        oa[8 * B :] = adds[0][...]
        ob[8 * B :] = adds[0][...]


def backward(chunk, tab, offs, tiles, d0, d1, adds=()):
    shape = (8 * B + B // 2, B) if chunk == 1 else (8, B, B)
    return pl.pallas_call(
        functools.partial(_backward_kernel, chunk, len(adds)),
        name=f"tiles_backward_{chunk}",
        in_specs=[SMEM, SMEM, HBM, VMEM, VMEM] + [VMEM] * len(adds),
        out_specs=[VMEM] * 2,
        out_shape=[jax.ShapeDtypeStruct(shape, BF16)] * 2,
        scratch_shapes=[
            pltpu.VMEM((16, B, B), F32),
            pltpu.VMEM((NBUF, B, B), BF16),
            pltpu.SemaphoreType.DMA((NBUF,)),
        ],
        compiler_params=pltpu.CompilerParams(vmem_limit_bytes=24 * MIB),
        cost_estimate=_cost(6 * MIB),
    )(tab, offs, tiles, d0, d1, *adds)


def _dense_kernel(near, far, cot0, cot1, w_ref, act, dagg, wterm):
    w = w_ref[...]
    for k in range(4):
        agg = (near[k].astype(F32) + far[(k + 2) % 4].astype(F32)).astype(BF16)
        pre = jnp.dot(agg, w, preferred_element_type=F32)
        sig = jax.nn.sigmoid(pre)
        cot = (cot0 if k < 2 else cot1)[k % 2].astype(F32)
        dpre = (cot * sig * (1.0 + pre * (1.0 - sig))).astype(BF16)
        dagg[k] = lax.dot_general(
            w, dpre, (((1,), (1,)), ((), ())), preferred_element_type=F32
        ).astype(BF16)
        term = lax.dot_general(agg, dpre, (((0,), (0,)), ((), ())), preferred_element_type=F32)
        if k < 2:
            act[k] = (pre * sig).astype(BF16)
        if k % 2 == 0:
            wterm[k // 2] = term
        else:
            wterm[k // 2] = wterm[k // 2] + term


def dense(near, far, cot0, cot1, w):
    return pl.pallas_call(
        _dense_kernel,
        name="dense",
        in_specs=[VMEM] * 5,
        out_specs=[VMEM] * 3,
        out_shape=[
            jax.ShapeDtypeStruct((2, B, B), BF16),
            jax.ShapeDtypeStruct((4, B, B), BF16),
            jax.ShapeDtypeStruct((2, B, B), F32),
        ],
        compiler_params=pltpu.CompilerParams(vmem_limit_bytes=16 * MIB),
        cost_estimate=pl.CostEstimate(
            flops=10 * 2 * B**3, bytes_accessed=5 * MIB, transcendentals=1024 * 256
        ),
    )(near, far, cot0, cot1, w)


def plus(*terms):
    total = terms[0].astype(F32)
    for t in terms[1:]:
        total = total + t.astype(F32)
    return total.astype(BF16)


def blocks(rows):
    return rows.reshape(-1, B, B)


def carry(value, w):
    return jnp.concatenate([value.reshape(-1, B), w])


def ring_sum(own, across, left, right, kind=BF16):
    own, across, left, right = (t.astype(F32) for t in (own, across, left, right))
    return ((own + across) + (left + right)).astype(kind)


def body(node_feats, weight, cotangent, tiles, tile_rows, tile_cols, tile_count):
    node, rep = lax.axis_index("node"), lax.axis_index("rep")
    x, yl, z = node % NX, node // NX % NYL, node // (NX * NYL)
    c, yh = rep % NC, rep // NC
    tiles = pltpu.with_memory_space_constraint(tiles[0, 0], pltpu.HBM)
    fwd, bwd, foffs, boffs = tables(
        tile_rows[0, 0], tile_cols[0, 0], tile_count[0, 0], z, yl, x, yh, c
    )
    own = lax.dynamic_slice_in_dim(node_feats.reshape(8, B, B), rep * 2, 2, 0)
    cot0 = cotangent.reshape(2, B, B)

    def ring(t):
        return jnp.concatenate([t, send(t, UP), send(t, UM), send(t, U2)])

    other = send(own, YN)
    lo, hi = ring(own), ring(other)
    cot1 = send(tie(cot0, other), YH)
    hi, cot1 = lax.optimization_barrier((hi, cot1))
    p1, m1 = send(lo, VP), send(lo, VM)
    p2, m2 = send(hi, VP), send(hi, VM)
    acc = forward(0, fwd, foffs, tiles, lo, hi, None)
    p1, m1, acc = lax.optimization_barrier((p1, m1, acc))
    p3 = send(p1, VP)
    acc = forward(1, fwd, foffs, tiles, p1, m1, acc)
    p2, m2, acc = lax.optimization_barrier((p2, m2, acc))
    m3 = send(m2, VM)
    acc = forward(2, fwd, foffs, tiles, p2, m2, acc)
    acc = forward(3, fwd, foffs, tiles, p3, m3, acc)

    core = send(acc[4:], CC)
    part = (acc[:4] + core).astype(BF16)
    across = send(part, YH)
    act, d0, term = dense(part, across, cot0, cot1, weight)

    half = B // 2
    whole = term[0] + term[1]
    keep = lax.dynamic_slice_in_dim(whole, c * half, half, 0)
    give = lax.dynamic_slice_in_dim(whole, (1 - c) * half, half, 0)
    d1, got = lax.optimization_barrier((send(d0, CC), send(give, CC)))
    w = (keep + got).astype(BF16)

    fa, fb = backward(3, bwd, boffs, tiles, d0, d1)
    ra, rb = send(fa, VP), send(fb, VM)
    d0, d1, fa, fb, w = lax.optimization_barrier((d0, d1, fa, fb, w))
    w2 = send(w, V2)
    m1, p1 = backward(1, bwd, boffs, tiles, d0, d1, (w,))
    s_hi, s_lo = send(p1, VP), send(m1, VM)
    d0, d1, m1, p1, ra, rb = lax.optimization_barrier((d0, d1, m1, p1, ra, rb))
    m2, p2 = backward(2, bwd, boffs, tiles, d0, d1, (rb, ra))
    t_lo, t_hi = send(p2, VP), send(m2, VM)
    d0, d1, m2, p2 = lax.optimization_barrier((d0, d1, m2, p2))
    lo, hi = backward(0, bwd, boffs, tiles, d0, d1)
    s_lo, s_hi, w2 = lax.optimization_barrier((s_lo, s_hi, w2))
    w = ring_sum(w, w2, s_hi[8 * B :], s_lo[8 * B :], F32)
    w = (w + send(w, YN)).astype(BF16)
    s_lo, s_hi = blocks(s_lo[: 8 * B]), blocks(s_hi[: 8 * B])
    def spread(own, s, t, extra):
        near, down, up, two = (plus(own[k : k + 2], s[k : k + 2], t[k : k + 2]) for k in (0, 2, 4, 6))
        if extra is not None:
            down, up, two = (carry(v, extra) for v in (down, up, two))
        return near, send(two, U2), send(up, UP), send(down, UM)

    far, *rest = spread(hi, s_hi, t_hi, w)
    near, *parts = spread(lo, s_lo, t_lo, None)
    far = plus(far, *(blocks(r[: 2 * B]) for r in rest))
    w = ring_sum(w, *(r[2 * B :] for r in rest), F32)
    other = send(far, YN)
    got = send(w, CC)
    total = sum((t.astype(F32) for t in (near, *parts, other)), jnp.zeros((), F32))
    feature_grad = jnp.swapaxes(total, 1, 2).astype(BF16).reshape(2 * B, B)
    scale = float(node_feats.shape[0] * NZ * NYL * NX) ** (-0.5)
    weight_grad = jnp.where(
        c == 0, jnp.concatenate([w, got]), jnp.concatenate([got, w])
    ) * scale
    return act.reshape(2 * B, B), feature_grad, weight_grad


def solution(mesh):
    placed = (
        P("node", None),
        P(),
        P(("node", "rep"), None),
        P("node", "rep", None, None, None),
        P("node", "rep", None),
        P("node", "rep", None),
        P("node", "rep"),
    )
    return jax.shard_map(
        body,
        mesh=mesh,
        in_specs=placed,
        out_specs=(P(("node", "rep"), None), P(("node", "rep"), None), P()),
        check_vma=False,
    )
```
